32 devices in a mesh: grp: 2 (over x), seq: 8 (over z, core), hd: 2 (over y).
Axes of the slice: x: 2, y: 2, z: 4, core: 2. Of those that a mesh axis runs over, the one named last changes fastest.
Arguments:
- latent_qkv: bfloat16 [2, 8, 256, 3, 3072], P('grp', 'seq', None, None, 'hd'), may hold values from -6 to 6
- cross_query: bfloat16 [2, 8, 256, 3072], P('grp', 'seq', None, 'hd'), may hold values from -6 to 6
- residual: bfloat16 [2, 8, 256, 3072], P('grp', 'seq', None, 'hd'), may hold values from -4 to 4
- prompt_states: bfloat16 [2, 512, 4096], P(None, 'seq', 'grp'), may hold values from -6 to 6
- kv_weight: bfloat16 [4096, 2, 3072], P(('grp', 'seq'), None, 'hd'), may hold values from -0.09375 to 0.09375, as said below
- prompt_lengths: int32 [2], replicated, may hold values from 32 to 512
- assignment: int32 [2], replicated, may hold values from 0 to 1, each once
Outputs:
- block_out: bfloat16 [2, 8, 256, 3072], P('grp', 'seq', None, 'hd')
The draws below stay inside these ranges and needn't reach their ends.
Inputs may be any that keep to these rules, and one draw needn't show every extreme that they name: Replica g serves prompt assignment[g]; every prompt is served by exactly one replica. `prompt_lengths`: key positions at or beyond a prompt's length are padding. `kv_weight`: entries have mean 0 and deviation 4096 ** -0.5.
All inputs are finite; a program needn't handle non-finite values.
Results may differ from the reference program's by a relative error of at most 0.0075.
Values may be sent and summed in bfloat16 or wider, within the bound.
No kernel may reach another device: no remote copies, remote signals or barrier semaphores. Data moves between devices by JAX's collectives and lax.ppermute only.
A program may use at most 64 MiB of HBM per device.

```python
import math
import jax
import jax.numpy as jnp
from jax import lax

D = 4096
HEADS = 24
HDIM = 128
PLEN = 512
SPATIAL = 256
DM = 3072
FRAMES = 8
PROMPTS = 2
N_GRP = 2


def clipped_normal(sub_key, dims):
    return jnp.clip(jax.random.normal(sub_key, dims, jnp.float32), -6.0, 6.0)


def weight_table(key):
    bound_value = 6.0 / math.sqrt(D)
    sampled = jax.random.normal(jax.random.fold_in(key, 101), (D, 2, DM), jnp.float32) / math.sqrt(D)
    sampled = jnp.clip(sampled, -bound_value, bound_value)
    return sampled.astype(jnp.bfloat16).astype(jnp.float32)


def draw_kv_weight(key, part):
    return weight_table(key).astype(jnp.bfloat16)


def draw_prompt_states(key, part):
    full_shape = (PROMPTS, PLEN, D)
    sampled = clipped_normal(jax.random.fold_in(key, 1), full_shape)
    return sampled.astype(jnp.bfloat16)


def draw_cross_query(key, part):
    full_shape = (N_GRP, FRAMES, SPATIAL, DM)
    sampled = clipped_normal(jax.random.fold_in(key, 2), full_shape)
    return sampled.astype(jnp.bfloat16)


def draw_latent_qkv(key, part):
    full_shape = (N_GRP, FRAMES, SPATIAL, 3, DM)
    sampled = clipped_normal(jax.random.fold_in(key, 3), full_shape)
    return sampled.astype(jnp.bfloat16)


def steps_of(key, shape, pieces, least, largest):
    level = 1.0
    for position, shards_of in pieces:
        draws = jax.random.uniform(jax.random.fold_in(jax.random.fold_in(key, 6), position), (shards_of,), jnp.float32, least / len(pieces), largest / len(pieces))
        level = level * jnp.repeat(jnp.exp(draws), shape[position] // shards_of).reshape((-1,) + (1,) * (len(shape) - 1 - position))
    return level


def gaussian(stream_key, shape, deviation, bound, cuts=(), held_as=jnp.bfloat16):
    entries = deviation * jax.random.normal(stream_key, shape, jnp.float32)
    if cuts:
        entries = entries * steps_of(stream_key, shape, cuts, -0.22, 0.18)
    return jnp.clip(entries, -bound, bound).astype(held_as)


def setup_inputs(seed: int = 0) -> dict:
    key_list = jax.random.split(jax.random.key(seed), 8)
    latent_qkv = draw_latent_qkv(jax.random.fold_in(key_list[7], 71), 0)
    cross_query = draw_cross_query(jax.random.fold_in(key_list[7], 71), 0)
    residual = gaussian(key_list[2], (N_GRP, FRAMES, SPATIAL, DM), 0.5, 4.0, ((0, 2), (1, 8), (3, 2)))
    prompt_states = draw_prompt_states(jax.random.fold_in(key_list[7], 71), 0)
    kv_weight = draw_kv_weight(jax.random.fold_in(key_list[7], 71), 0)
    prompt_lengths = jax.random.randint(key_list[5], (PROMPTS,), max(1, PLEN // 16), PLEN + 1).astype(jnp.int32)
    assignment = jax.random.permutation(key_list[6], N_GRP).astype(jnp.int32)
    return dict(latent_qkv=latent_qkv, cross_query=cross_query, residual=residual, prompt_states=prompt_states, kv_weight=kv_weight, prompt_lengths=prompt_lengths, assignment=assignment)


def attend(queries, key_rows, values, key_bias):
    scores = jnp.einsum('qhe,khe->hqk', queries.astype(jnp.float32), key_rows.astype(jnp.float32))
    scores = scores / math.sqrt(queries.shape[-1]) + key_bias
    row_max = lax.optimization_barrier(jnp.max(scores, axis=-1, keepdims=True))
    powered = jnp.exp(scores - row_max)
    weights = (powered / lax.optimization_barrier(jnp.sum(powered, axis=-1, keepdims=True))).astype(jnp.bfloat16)
    return jnp.einsum('hqk,khe->qhe', weights.astype(jnp.float32), values.astype(jnp.float32))

def reference(latent_qkv, cross_query, residual, prompt_states, kv_weight, prompt_lengths, assignment):

    def one_group(group_index):
        chosen = assignment[group_index]
        prompt = prompt_states[chosen]
        pairs = jnp.dot(prompt, kv_weight.reshape(D, 2 * DM), preferred_element_type=jnp.float32)
        pairs = pairs.astype(jnp.bfloat16).reshape(PLEN, 2, HEADS, HDIM)
        key_bias = jnp.where(jnp.arange(PLEN) < prompt_lengths[chosen], 0.0, -1000000000.0).astype(jnp.float32)
        latent = latent_qkv[group_index].reshape(FRAMES, SPATIAL, 3, HEADS, HDIM)
        crossing = cross_query[group_index].reshape(FRAMES, SPATIAL, HEADS, HDIM)

        def one_frame(frame_index):
            local = latent[frame_index]
            spatial_out = attend(local[:, 0], local[:, 1], local[:, 2], jnp.float32(0.0))
            cross_out = attend(crossing[frame_index], pairs[:, 0], pairs[:, 1], key_bias)
            return spatial_out + cross_out
        framewise = lax.map(one_frame, jnp.arange(FRAMES))
        scores = jnp.einsum('fnhe,gnhe->nhfg', latent[:, :, 0].astype(jnp.float32), latent[:, :, 1].astype(jnp.float32))
        scores = scores / math.sqrt(HDIM)
        row_max = lax.optimization_barrier(jnp.max(scores, axis=-1, keepdims=True))
        powered = jnp.exp(scores - row_max)
        weights = (powered / lax.optimization_barrier(jnp.sum(powered, axis=-1, keepdims=True))).astype(jnp.bfloat16)
        temporal = jnp.einsum('nhfg,gnhe->fnhe', weights.astype(jnp.float32), latent[:, :, 2].astype(jnp.float32))
        temporal = temporal.astype(jnp.bfloat16).astype(jnp.float32)
        total = residual[group_index].astype(jnp.float32) + framewise.reshape(FRAMES, SPATIAL, DM)
        total = total + temporal.reshape(FRAMES, SPATIAL, DM)
        return total.astype(jnp.bfloat16)
    return lax.map(one_group, jnp.arange(N_GRP))
```

```python
import functools
import math

import jax
import jax.numpy as jnp
from jax import lax
from jax.experimental import pallas as pl
from jax.experimental.pallas import tpu as pltpu
from jax.sharding import PartitionSpec as P

HDIM = 128
BF16 = jnp.bfloat16
F32 = jnp.float32


def swap(value, axis, bit):
    pairs = [(i, i ^ bit) for i in range(lax.axis_size(axis))]
    return lax.ppermute(value, axis, pairs)


def pick(stacked, index):
    return lax.dynamic_index_in_dim(stacked, index, 0, keepdims=False)


def scores_of(queries, key_rows):
    scores = lax.dot_general(queries, key_rows, (((1,), (1,)), ((), ())), preferred_element_type=F32)
    return scores * (1.0 / math.sqrt(HDIM))


def weigh(scores, values):
    powered = jnp.exp(scores - jnp.max(scores, axis=-1, keepdims=True))
    weights = (powered * (1.0 / jnp.sum(powered, axis=-1, keepdims=True))).astype(BF16)
    return jnp.dot(weights, values, preferred_element_type=F32)


def lanes(head):
    return slice(head * HDIM, (head + 1) * HDIM)


def block_heads(heads, most):
    return max(n for n in range(1, most + 1) if heads % n == 0)


def spatial_kernel(qkv_ref, residual_ref, out_ref):
    for head in range(out_ref.shape[1] // HDIM):
        at = lanes(head)
        result = weigh(scores_of(qkv_ref[0, :, at], qkv_ref[1, :, at]), qkv_ref[2, :, at])
        out_ref[:, at] = residual_ref[:, at].astype(F32) + result


def spatial_attention(qkv, residual):
    _, tokens, width = qkv.shape
    cols = HDIM * block_heads(width // HDIM, 3)
    return pl.pallas_call(
        spatial_kernel,
        grid=(width // cols,),
        in_specs=[
            pl.BlockSpec((3, tokens, cols), lambda j: (0, 0, j)),
            pl.BlockSpec((tokens, cols), lambda j: (0, j)),
        ],
        out_specs=pl.BlockSpec((tokens, cols), lambda j: (0, j)),
        out_shape=jax.ShapeDtypeStruct((tokens, width), F32),
        name="spatial",
    )(qkv, residual)


def temporal_kernel(qkv_ref, out_ref):
    frames, _, tokens, cols = qkv_ref.shape
    rows = frames * tokens
    row_token = lax.rem(lax.broadcasted_iota(jnp.int32, (rows, rows), 0), tokens)
    col_token = lax.rem(lax.broadcasted_iota(jnp.int32, (rows, rows), 1), tokens)
    same = row_token == col_token
    for head in range(cols // HDIM):
        at = lanes(head)
        query, key_rows, values = (qkv_ref[:, i, :, at].reshape(rows, HDIM) for i in range(3))
        scores = jnp.where(same, scores_of(query, key_rows), -jnp.inf)
        result = weigh(scores, values).astype(BF16)
        out_ref[:, :, at] = result.reshape(frames, tokens, HDIM)


def temporal_attention(qkv):
    frames, _, tokens, width = qkv.shape
    cols = HDIM * block_heads(width // HDIM, 3)
    return pl.pallas_call(
        temporal_kernel,
        grid=(width // cols,),
        in_specs=[pl.BlockSpec((frames, 3, tokens, cols), lambda j: (0, 0, 0, j))],
        out_specs=pl.BlockSpec((frames, tokens, cols), lambda j: (0, 0, j)),
        out_shape=jax.ShapeDtypeStruct((frames, tokens, width), BF16),
        name="temporal",
    )(qkv)


def cross_kernel(pieces, scalar_ref, own_q_ref, far_q_ref, *refs):
    key_refs, value_refs = refs[:pieces], refs[pieces : 2 * pieces]
    own_ref, far_ref = refs[2 * pieces :]
    tokens = own_q_ref.shape[0]
    each = key_refs[0].shape[0]
    place = lax.broadcasted_iota(jnp.int32, (1, each), 1)
    limit = scalar_ref[0]
    bias = jnp.concatenate(
        [jnp.where(place + scalar_ref[1 + i] * each < limit, 0.0, -1e9) for i in range(pieces)], axis=1
    ).astype(F32)
    for head in range(own_q_ref.shape[1] // HDIM):
        at = lanes(head)
        query = jnp.concatenate([own_q_ref[:, at], far_q_ref[:, at]], axis=0)
        key_rows = jnp.concatenate([r[:, at] for r in key_refs], axis=0)
        values = jnp.concatenate([r[:, at] for r in value_refs], axis=0)
        result = weigh(scores_of(query, key_rows) + bias, values)
        own_ref[:, at] = result[:tokens]
        far_ref[:, at] = result[tokens:].astype(BF16)


def cross_attention(scalars, own_q, far_q, pieces):
    tokens, width = own_q.shape
    cols = HDIM * block_heads(width // HDIM, 3)
    steps = width // cols
    each = pieces[0].shape[0]
    n = len(pieces)
    q_spec = pl.BlockSpec((tokens, cols), lambda j, s: (0, j))
    return pl.pallas_call(
        functools.partial(cross_kernel, n),
        grid_spec=pltpu.PrefetchScalarGridSpec(
            num_scalar_prefetch=1,
            grid=(steps,),
            in_specs=[q_spec, q_spec]
            + [pl.BlockSpec((each, cols), lambda j, s: (0, j))] * n
            + [pl.BlockSpec((each, cols), lambda j, s: (0, steps + j))] * n,
            out_specs=[q_spec, q_spec],
        ),
        out_shape=[
            jax.ShapeDtypeStruct((tokens, width), F32),
            jax.ShapeDtypeStruct((tokens, width), BF16),
        ],
        name="cross",
    )(scalars, own_q, far_q, *pieces, *pieces)


def final_kernel(scalar_ref, base_ref, temporal_ref, own_ref, far_ref, out_ref):
    partial = base_ref[...] + temporal_ref[...].astype(F32)

    @pl.when(pl.program_id(0) == 0)
    def _():
        out_ref[...] = (partial + own_ref[...]).astype(BF16)

    @pl.when(pl.program_id(0) == 1)
    def _():
        out_ref[...] = (partial + far_ref[...].astype(F32)).astype(BF16)


def final_sum(core, base, temporal, own, far):
    tokens, width = base.shape
    half = width // 2
    side = pl.BlockSpec((tokens, half), lambda j, s: (0, j ^ s[0]))
    whole = pl.BlockSpec((tokens, half), lambda j, s: (0, 0))
    return pl.pallas_call(
        final_kernel,
        grid_spec=pltpu.PrefetchScalarGridSpec(
            num_scalar_prefetch=1, grid=(2,), in_specs=[side, side, whole, whole], out_specs=side
        ),
        out_shape=jax.ShapeDtypeStruct((tokens, width), BF16),
        name="final",
    )(core.reshape(1), base, temporal, own, far)


def body(latent_qkv, cross_query, residual, prompt_states, kv_weight, prompt_lengths, assignment):
    tokens, width = cross_query.shape[2:]
    half = width // 2
    seq, grp = lax.axis_size("seq"), lax.axis_size("grp")
    me, group = lax.axis_index("seq"), lax.axis_index("grp")
    core = me & 1
    chips = seq // 2
    bits = chips.bit_length() - 1
    feats = kv_weight.shape[0]

    prompts, rows_here, _ = prompt_states.shape
    parts = prompt_states.reshape(prompts, rows_here, seq, feats).transpose(2, 0, 1, 3)
    parts = lax.all_to_all(parts, "seq", 0, 0, tiled=True)
    rows = seq * rows_here

    qkv = latent_qkv[0, 0].transpose(1, 0, 2)
    blocks = qkv.reshape(3, seq, tokens // seq, width).transpose(1, 0, 2, 3)
    frames = lax.all_to_all(blocks, "seq", 0, 0, tiled=True)

    halves = kv_weight.reshape(feats, 2, 2, half).transpose(2, 0, 1, 3).reshape(2, feats, width)
    weight = [pick(halves, core), swap(pick(halves, 1 - core), "seq", 1)]
    weight = jnp.concatenate(weight, axis=0)
    weights = [weight] + [swap(weight, "grp", k) for k in range(1, grp)]

    slots = jnp.take(assignment, group ^ jnp.arange(grp))
    wanted = [parts[:, slots[k]].reshape(rows, feats) for k in range(grp)]
    wanted = [wanted[0]] + [swap(wanted[k], "grp", k) for k in range(1, grp)]
    wanted = jnp.stack(wanted)
    near = swap(wanted, "seq", 1)
    states = jnp.concatenate([w for k in range(grp) for w in (wanted[k], near[k])], axis=1)
    total = jnp.dot(states, jnp.concatenate(weights, axis=0), preferred_element_type=F32)

    for bit in range(bits):
        if bit < bits - 1:
            mine = (me >> (bit + 1)) & 1
            total = total.reshape(2, total.shape[0] // 2, width)
            kept, sent = pick(total, mine), pick(total, 1 - mine)
        else:
            kept = sent = total
        total = kept + swap(sent.astype(BF16), "seq", 2 << bit).astype(F32)
    pieces = [total.astype(BF16)]
    place = jnp.int32(0)
    for bit in range(bits - 1):
        place = place * 2 + ((me >> (bit + 1)) & 1)
    places = [place]
    for bit in reversed(range(bits - 1)):
        pieces = pieces + [swap(p, "seq", 2 << bit) for p in pieces]
        places = places + [p ^ (1 << (bits - 2 - bit)) for p in places]

    length = jnp.take(prompt_lengths, jnp.take(assignment, group))
    scalars = jnp.stack([length] + places).astype(jnp.int32)
    query = cross_query[0, 0].reshape(tokens, 2, half).transpose(1, 0, 2)
    far_q = swap(pick(query, 1 - core), "seq", 1)
    own, far = cross_attention(scalars, pick(query, core), far_q, pieces)
    far = swap(far, "seq", 1)

    base = spatial_attention(qkv, residual[0, 0])
    temporal = temporal_attention(frames)
    temporal = lax.all_to_all(temporal, "seq", 0, 0, tiled=True).reshape(tokens, width)
    return final_sum(core, base, temporal, own, far)[None, None]


def solution(mesh):
    return jax.shard_map(
        body,
        mesh=mesh,
        in_specs=(
            P("grp", "seq", None, None, "hd"),
            P("grp", "seq", None, "hd"),
            P("grp", "seq", None, "hd"),
            P(None, "seq", "grp"),
            P(("grp", "seq"), None, "hd"),
            P(),
            P(),
        ),
        out_specs=P("grp", "seq", None, "hd"),
        check_vma=False,
    )
```

```python
import functools
import math

import jax
import jax.numpy as jnp
from jax import lax
from jax.experimental import pallas as pl
from jax.experimental.pallas import tpu as pltpu
from jax.sharding import PartitionSpec as P


HDIM = 128
BF16 = jnp.bfloat16
F32 = jnp.float32


def swap(value, axis, bits):
    pairs = [(i, i ^ bits) for i in range(lax.axis_size(axis))]
    return lax.ppermute(value, axis, pairs)


def scores_of(queries, key_rows):
    scores = lax.dot_general(queries, key_rows, (((1,), (1,)), ((), ())), preferred_element_type=F32)
    return scores * (1.0 / math.sqrt(HDIM))


def softmax(scores):
    powered = jnp.exp(scores - jnp.max(scores, axis=-1, keepdims=True))
    return (powered * (1.0 / jnp.sum(powered, axis=-1, keepdims=True))).astype(BF16)


def lanes(head):
    return slice(head * HDIM, (head + 1) * HDIM)


def block_cols(width, most=3):
    heads = width // HDIM
    return HDIM * max(n for n in range(1, most + 1) if heads % n == 0)


def prompt_kernel(scalar_ref, in_ref, out_ref):
    out_ref[0] = in_ref[...]


def prompt_blocks(states, side, sides, blocks):
    prompts, rows, feats = states.shape
    rows, feats = rows // sides, feats // blocks
    if feats % HDIM:
        cut = lax.dynamic_slice_in_dim(states, side * rows, rows, 1)
        return cut.reshape(prompts, rows, blocks, feats).transpose(2, 0, 1, 3)
    return pl.pallas_call(
        prompt_kernel,
        grid_spec=pltpu.PrefetchScalarGridSpec(
            num_scalar_prefetch=1,
            grid=(blocks,),
            in_specs=[pl.BlockSpec((prompts, rows, feats), lambda j, s: (0, s[0], j))],
            out_specs=pl.BlockSpec((1, prompts, rows, feats), lambda j, s: (j, 0, 0, 0)),
        ),
        out_shape=jax.ShapeDtypeStruct((blocks, prompts, rows, feats), BF16),
        name="prompt_blocks",
    )(side.reshape(1), states)


def project_kernel(n_rows, n_grp, scalar_ref, *refs):
    state_refs = refs[: 2 * n_rows]
    weight_refs = refs[2 * n_rows : 2 * n_rows + n_grp]
    kept_ref, sent_ref = refs[2 * n_rows + n_grp :]
    rows = state_refs[0].shape[1]
    first = pl.program_id(0) == 0
    for i in range(n_rows):
        total = None
        for core in range(2):
            for g in range(n_grp):
                part = jnp.dot(
                    state_refs[2 * i + core][g], weight_refs[g][core], preferred_element_type=F32
                )
                total = part if total is None else total + part

        @pl.when(first)
        def _(total=total, i=i):
            kept_ref[i * rows : (i + 1) * rows, :] = total

        @pl.when(jnp.logical_not(first))
        def _(total=total, i=i):
            sent_ref[i * rows : (i + 1) * rows, :] = total.astype(BF16)


def project(states, weights, near):
    n_grp, rows, feats = states[0].shape
    n_rows = len(states) // 2
    cols = weights[0].shape[2] // 2
    whole = pl.BlockSpec((n_grp, rows, feats), lambda j, s: (0, 0, 0))
    side = pl.BlockSpec((2, feats, cols), lambda j, s: (0, 0, j ^ s[0]))
    out = pl.BlockSpec((n_rows * rows, cols), lambda j, s: (0, 0))
    return pl.pallas_call(
        functools.partial(project_kernel, n_rows, n_grp),
        grid_spec=pltpu.PrefetchScalarGridSpec(
            num_scalar_prefetch=1,
            grid=(2,),
            in_specs=[whole] * len(states) + [side] * n_grp,
            out_specs=[out, out],
        ),
        out_shape=[
            jax.ShapeDtypeStruct((n_rows * rows, cols), F32),
            jax.ShapeDtypeStruct((n_rows * rows, cols), BF16),
        ],
        name="project",
    )(near.reshape(1), *states, *weights)


def spatial_kernel(qkv_ref, residual_ref, out_ref):
    for head in range(out_ref.shape[1] // HDIM):
        at = lanes(head)
        weights = softmax(scores_of(qkv_ref[0, :, at], qkv_ref[1, :, at]))
        result = jnp.dot(weights, qkv_ref[2, :, at], preferred_element_type=F32)
        out_ref[:, at] = residual_ref[:, at].astype(F32) + result


def spatial_attention(qkv, residual):
    _, tokens, width = qkv.shape
    cols = block_cols(width)
    return pl.pallas_call(
        spatial_kernel,
        grid=(width // cols,),
        in_specs=[
            pl.BlockSpec((3, tokens, cols), lambda j: (0, 0, j)),
            pl.BlockSpec((tokens, cols), lambda j: (0, j)),
        ],
        out_specs=pl.BlockSpec((tokens, cols), lambda j: (0, j)),
        out_shape=jax.ShapeDtypeStruct((tokens, width), F32),
        name="spatial",
    )(qkv, residual)


def temporal_kernel(frames, scalar_ref, *refs):
    frame_refs, out_ref = refs[:frames], refs[frames]
    _, tokens, cols = frame_refs[0].shape
    rows = frames * tokens
    row_token = lax.rem(lax.broadcasted_iota(jnp.int32, (rows, rows), 0), tokens)
    col_token = lax.rem(lax.broadcasted_iota(jnp.int32, (rows, rows), 1), tokens)
    same = row_token == col_token
    for head in range(cols // HDIM):
        at = lanes(head)
        query, key_rows, values = (
            jnp.concatenate([r[i, :, at] for r in frame_refs], axis=0) for i in range(3)
        )
        weights = softmax(jnp.where(same, scores_of(query, key_rows), -jnp.inf))
        result = jnp.dot(weights, values, preferred_element_type=F32).astype(BF16)
        for j in range(frames):
            out_ref[scalar_ref[j], :, at] = result[j * tokens : (j + 1) * tokens]


def temporal_attention(places, pieces):
    frames = len(pieces)
    _, tokens, width = pieces[0].shape
    cols = block_cols(width)
    return pl.pallas_call(
        functools.partial(temporal_kernel, frames),
        grid_spec=pltpu.PrefetchScalarGridSpec(
            num_scalar_prefetch=1,
            grid=(width // cols,),
            in_specs=[pl.BlockSpec((3, tokens, cols), lambda j, s: (0, 0, j))] * frames,
            out_specs=pl.BlockSpec((frames, tokens, cols), lambda j, s: (0, 0, j)),
        ),
        out_shape=jax.ShapeDtypeStruct((frames, tokens, width), BF16),
        name="temporal",
    )(places, *pieces)


def weigh_kernel(bias_ref, kept_ref, come_ref, *refs):
    query_refs, out_ref = refs[:-1], refs[-1]
    key_rows = (kept_ref[...] + come_ref[...].astype(F32)).astype(BF16)
    for j, query_ref in enumerate(query_refs):
        scores = scores_of(query_ref[...], key_rows) + bias_ref[...]
        out_ref[0, j] = softmax(scores)


def cross_weights(bias, kept, come, queries):
    rows, width = kept.shape
    tokens = queries[0].shape[0]
    heads = width // HDIM
    key_spec = pl.BlockSpec((rows, HDIM), lambda h: (0, h))
    return pl.pallas_call(
        weigh_kernel,
        grid=(heads,),
        in_specs=[pl.BlockSpec((1, rows), lambda h: (0, 0)), key_spec, key_spec]
        + [pl.BlockSpec((tokens, HDIM), lambda h: (0, h))] * len(queries),
        out_specs=pl.BlockSpec((1, len(queries), tokens, rows), lambda h: (h, 0, 0, 0)),
        out_shape=jax.ShapeDtypeStruct((heads, len(queries), tokens, rows), BF16),
        name="cross_weights",
    )(bias, kept, come, *queries)


def value_kernel(weight_ref, kept_ref, come_ref, *out_refs):
    values = (kept_ref[...] + come_ref[...].astype(F32)).astype(BF16)
    for j, out_ref in enumerate(out_refs):
        result = jnp.dot(weight_ref[0, j], values, preferred_element_type=F32)
        out_ref[...] = result.astype(out_ref.dtype)


def cross_values(weights, kept, come):
    rows, width = kept.shape
    heads, count, tokens, _ = weights.shape
    key_spec = pl.BlockSpec((rows, HDIM), lambda h: (0, h))
    return pl.pallas_call(
        value_kernel,
        grid=(heads,),
        in_specs=[pl.BlockSpec((1, count, tokens, rows), lambda h: (h, 0, 0, 0)), key_spec, key_spec],
        out_specs=[pl.BlockSpec((tokens, HDIM), lambda h: (0, h))] * count,
        out_shape=[jax.ShapeDtypeStruct((tokens, width), F32 if j == 0 else BF16) for j in range(count)],
        name="cross_values",
    )(weights, kept, come)


def final_kernel(scalar_ref, base_ref, temporal_ref, *refs):
    piece_refs, out_ref = refs[:-1], refs[-1]
    partial = base_ref[...] + temporal_ref[...].astype(F32)
    for j, piece_ref in enumerate(piece_refs):

        @pl.when(pl.program_id(0) == j)
        def _(piece_ref=piece_ref):
            out_ref[...] = (partial + piece_ref[...].astype(F32)).astype(BF16)


def final_sum(place, base, temporal, pieces):
    tokens, width = base.shape
    cols = width // len(pieces)
    side = pl.BlockSpec((tokens, cols), lambda j, s: (0, j ^ s[0]))
    whole = pl.BlockSpec((tokens, cols), lambda j, s: (0, 0))
    return pl.pallas_call(
        final_kernel,
        grid_spec=pltpu.PrefetchScalarGridSpec(
            num_scalar_prefetch=1,
            grid=(len(pieces),),
            in_specs=[side, side] + [whole] * len(pieces),
            out_specs=side,
        ),
        out_shape=jax.ShapeDtypeStruct((tokens, width), BF16),
        name="final",
    )(place.reshape(1), base, temporal, *pieces)


def temporal_plan(seq):
    if seq != 8:
        return [(k, k) for k in range(seq - 1, 0, -1)]
    return [(6, 2), (2, 6), (7, 3), (3, 7), (4, 4), (5, 5), (1, 1)]


def block(latent_qkv, cross_query, residual, prompt_states, kv_weight, prompt_lengths, assignment):
    tokens, width = cross_query.shape[2:]
    seq, grp, sides = (lax.axis_size(name) for name in ("seq", "grp", "hd"))
    me, group, side = (lax.axis_index(name) for name in ("seq", "grp", "hd"))
    core, near = me & 1, (me >> 1) & 1
    place = core * 2 + near
    feats = kv_weight.shape[0]
    _, rows_here, _ = prompt_states.shape
    rows_side = rows_here // sides
    rows = seq * rows_side

    parts = prompt_blocks(prompt_states, side, sides, seq)
    parts = lax.all_to_all(parts, "seq", 0, 0, tiled=True)

    qkv = latent_qkv[0, 0].transpose(1, 0, 2)
    share = tokens // seq
    steps = temporal_plan(seq)
    own_block = lax.dynamic_slice_in_dim(qkv, me * share, share, 1)
    pieces, sources = [own_block], [me]
    for even, odd in steps:
        crossing = even & 1
        target = me ^ jnp.where(core == 0, even, odd)
        block = lax.dynamic_slice_in_dim(qkv, target * share, share, 1)
        pairs = [(i, i ^ (odd if i & 1 else even)) for i in range(seq)]
        pieces.append(lax.ppermute(block, "seq", pairs))
        sender_core = core ^ crossing
        sources.append(me ^ jnp.where(sender_core == 0, even, odd))

    half = width // 2
    weights = []
    for kind in range(2):
        plane = kv_weight[:, kind]
        mine = lax.dynamic_slice_in_dim(plane, core * half, half, 1)
        theirs = lax.dynamic_slice_in_dim(plane, (1 - core) * half, half, 1)
        come = swap(theirs, "seq", 1)
        both = jnp.stack([mine, come])
        weights.append([both] + [swap(both, "grp", k) for k in range(1, grp)])

    def slot(k):
        index = jnp.take(assignment, group ^ k)
        return lax.dynamic_index_in_dim(parts, index, 1, keepdims=False).reshape(rows, feats)

    wanted = jnp.stack([slot(0)] + [swap(slot(k), "grp", k) for k in range(1, grp)])
    n_pairs = [(s, h) for s in range(seq) for h in range(sides)]
    states = []
    for k in range(sides):
        for c in range(2):
            pairs = [(s * sides + h, (s ^ c) * sides + (h ^ k)) for s, h in n_pairs]
            states.append(wanted if k + c == 0 else lax.ppermute(wanted, ("seq", "hd"), pairs))

    quarter = width // 4
    query = cross_query[0, 0]
    queries = []
    for k, other in enumerate((0, 2, 1, 3)):
        block = lax.dynamic_slice_in_dim(query, (place ^ other) * quarter, quarter, 1)
        queries.append(block if k == 0 else swap(block, "seq", k))

    sums = []
    for kind in range(2):
        kept, sent = project(states, weights[kind], near)
        kept = kept + swap(sent, "seq", 2).astype(F32)
        bit = 4
        while bit < seq:
            come = swap(kept.astype(BF16), "seq", bit)
            bit *= 2
            if bit < seq:
                kept = kept + come.astype(F32)
        sums.append((kept, come))

    row = jnp.arange(rows * sides)
    which, source, inner = row // rows, (row % rows) // rows_side, row % rows_side
    position = source * rows_here + (which ^ side) * rows_side + inner
    length = jnp.take(prompt_lengths, jnp.take(assignment, group))
    bias = jnp.where(position < length, 0.0, -1e9).astype(F32)[None]

    base = spatial_attention(qkv, residual[0, 0])
    temporal = temporal_attention(jnp.stack(sources).astype(jnp.int32), pieces)
    temporal = lax.all_to_all(temporal, "seq", 0, 0, tiled=True).reshape(tokens, width)

    shares = cross_weights(bias, *sums[0], queries)
    crossed = cross_values(shares, *sums[1])
    results = [crossed[0]]
    for k in range(1, 4):
        results.append(swap(crossed[k], "seq", k))
    results[1], results[2] = results[2], results[1]
    return final_sum(place, base, temporal, results)[None, None]


def solution(mesh):
    return jax.shard_map(
        block,
        mesh=mesh,
        in_specs=(
            P("grp", "seq", None, None, "hd"),
            P("grp", "seq", None, "hd"),
            P("grp", "seq", None, "hd"),
            P(None, "seq", "grp"),
            P(("grp", "seq"), None, "hd"),
            P(),
            P(),
        ),
        out_specs=P("grp", "seq", None, "hd"),
        check_vma=False,
    )
```

```python
import functools
import math

import jax
import jax.numpy as jnp
from jax import lax
from jax.experimental import pallas as pl
from jax.experimental.pallas import tpu as pltpu
from jax.sharding import PartitionSpec as P


HDIM = 128
BF16 = jnp.bfloat16
F32 = jnp.float32


def swap(value, axis, bits):
    pairs = [(i, i ^ bits) for i in range(lax.axis_size(axis))]
    return lax.ppermute(value, axis, pairs)


def scores_of(queries, key_rows):
    scores = lax.dot_general(queries, key_rows, (((1,), (1,)), ((), ())), preferred_element_type=F32)
    return scores * (1.0 / math.sqrt(HDIM))


def softmax(scores):
    powered = jnp.exp(scores - jnp.max(scores, axis=-1, keepdims=True))
    return (powered * (1.0 / jnp.sum(powered, axis=-1, keepdims=True))).astype(BF16)


def lanes(head):
    return slice(head * HDIM, (head + 1) * HDIM)


def block_cols(width, most=3):
    heads = width // HDIM
    return HDIM * max(n for n in range(1, most + 1) if heads % n == 0)


def prompt_kernel(scalar_ref, in_ref, out_ref):
    blocks, _, _, feats = out_ref.shape
    for j in range(blocks):
        out_ref[j] = in_ref[:, :, j * feats : (j + 1) * feats]


def prompt_blocks(states, side, sides, blocks):
    prompts, rows, width = states.shape
    rows, feats = rows // sides, width // blocks
    if feats % HDIM:
        cut = lax.dynamic_slice_in_dim(states, side * rows, rows, 1)
        return cut.reshape(prompts, rows, blocks, feats).transpose(2, 0, 1, 3)
    shape = (blocks, prompts, rows, feats)
    return pl.pallas_call(
        prompt_kernel,
        grid_spec=pltpu.PrefetchScalarGridSpec(
            num_scalar_prefetch=1,
            grid=(1,),
            in_specs=[pl.BlockSpec((prompts, rows, width), lambda j, s: (0, s[0], 0))],
            out_specs=pl.BlockSpec(shape, lambda j, s: (0, 0, 0, 0)),
        ),
        out_shape=jax.ShapeDtypeStruct(shape, BF16),
        name="prompt_blocks",
    )(side.reshape(1), states)


def project_kernel(n_rows, scalar_ref, *refs):
    near = scalar_ref[0]
    state_refs = refs[: 2 * n_rows]
    kept_ref, sent_ref = refs[-2:]
    weight_refs = refs[2 * n_rows : -2]
    rows, cols = state_refs[0].shape[1], kept_ref.shape[1]

    def product(i, start):
        total = None
        for j, weight_ref in enumerate(weight_refs):
            state = state_refs[2 * i + j % 2][j // 2]
            weight = weight_ref[:, pl.ds(pl.multiple_of(start, HDIM), cols)]
            part = jnp.dot(state, weight, preferred_element_type=F32)
            total = part if total is None else total + part
        return total

    for i in range(n_rows):
        sent_ref[i * rows : (i + 1) * rows, :] = product(i, (1 - near) * cols).astype(BF16)
    for i in range(n_rows):
        kept_ref[i * rows : (i + 1) * rows, :] = product(i, near * cols)


VMEM_SPEC = pl.BlockSpec(memory_space=pltpu.VMEM)
SMEM_SPEC = pl.BlockSpec(memory_space=pltpu.SMEM)


def project(states, weights, near):
    _, rows, _ = states[0].shape
    n_rows = len(states) // 2
    shape = (n_rows * rows, weights[0].shape[1] // 2)
    return pl.pallas_call(
        functools.partial(project_kernel, n_rows),
        in_specs=[SMEM_SPEC] + [VMEM_SPEC] * (len(states) + len(weights)),
        out_specs=[VMEM_SPEC] * 2,
        out_shape=[jax.ShapeDtypeStruct(shape, F32), jax.ShapeDtypeStruct(shape, BF16)],
        name="project",
    )(near.reshape(1), *states, *weights)


def spatial_kernel(qkv_ref, residual_ref, out_ref):
    for head in range(out_ref.shape[1] // HDIM):
        at = lanes(head)
        weights = softmax(scores_of(qkv_ref[0, :, at], qkv_ref[1, :, at]))
        result = jnp.dot(weights, qkv_ref[2, :, at], preferred_element_type=F32)
        out_ref[:, at] = residual_ref[:, at].astype(F32) + result


def spatial_attention(qkv, residual):
    _, tokens, width = qkv.shape
    cols = block_cols(width)
    return pl.pallas_call(
        spatial_kernel,
        grid=(width // cols,),
        in_specs=[
            pl.BlockSpec((3, tokens, cols), lambda j: (0, 0, j)),
            pl.BlockSpec((tokens, cols), lambda j: (0, j)),
        ],
        out_specs=pl.BlockSpec((tokens, cols), lambda j: (0, j)),
        out_shape=jax.ShapeDtypeStruct((tokens, width), F32),
        name="spatial",
    )(qkv, residual)


def temporal_kernel(frames, scalar_ref, *refs):
    frame_refs, out_ref = refs[:frames], refs[frames]
    _, tokens, cols = frame_refs[0].shape
    rows = frames * tokens
    row_token = lax.rem(lax.broadcasted_iota(jnp.int32, (rows, rows), 0), tokens)
    col_token = lax.rem(lax.broadcasted_iota(jnp.int32, (rows, rows), 1), tokens)
    same = row_token == col_token
    for head in range(cols // HDIM):
        at = lanes(head)
        query, key_rows, values = (
            jnp.concatenate([r[i, :, at] for r in frame_refs], axis=0) for i in range(3)
        )
        weights = softmax(jnp.where(same, scores_of(query, key_rows), -jnp.inf))
        result = jnp.dot(weights, values, preferred_element_type=F32).astype(BF16)
        for j in range(frames):
            out_ref[scalar_ref[j], :, at] = result[j * tokens : (j + 1) * tokens]


def temporal_attention(places, pieces):
    frames = len(pieces)
    _, tokens, width = pieces[0].shape
    cols = block_cols(width)
    return pl.pallas_call(
        functools.partial(temporal_kernel, frames),
        grid_spec=pltpu.PrefetchScalarGridSpec(
            num_scalar_prefetch=1,
            grid=(width // cols,),
            in_specs=[pl.BlockSpec((3, tokens, cols), lambda j, s: (0, 0, j))] * frames,
            out_specs=pl.BlockSpec((frames, tokens, cols), lambda j, s: (0, 0, j)),
        ),
        out_shape=jax.ShapeDtypeStruct((frames, tokens, width), BF16),
        name="temporal",
    )(places, *pieces)


def weigh_kernel(bias_ref, kept_ref, come_ref, *refs):
    query_refs, out_ref = refs[:-1], refs[-1]
    for head in range(out_ref.shape[0]):
        at = lanes(head)
        key_rows = (kept_ref[:, at] + come_ref[:, at].astype(F32)).astype(BF16)
        for j, query_ref in enumerate(query_refs):
            out_ref[head, j] = softmax(scores_of(query_ref[:, at], key_rows) + bias_ref[...])


def cross_weights(bias, kept, come, queries):
    rows, width = kept.shape
    tokens = queries[0].shape[0]
    return pl.pallas_call(
        weigh_kernel,
        in_specs=[VMEM_SPEC] * (3 + len(queries)),
        out_specs=VMEM_SPEC,
        out_shape=jax.ShapeDtypeStruct((width // HDIM, len(queries), tokens, rows), BF16),
        name="cross_weights",
    )(bias, kept, come, *queries)


def value_kernel(weight_ref, kept_ref, come_ref, *out_refs):
    for head in range(weight_ref.shape[0]):
        at = lanes(head)
        values = (kept_ref[:, at] + come_ref[:, at].astype(F32)).astype(BF16)
        for j, out_ref in enumerate(out_refs):
            result = jnp.dot(weight_ref[head, j], values, preferred_element_type=F32)
            out_ref[:, at] = result.astype(out_ref.dtype)


def cross_values(weights, kept, come):
    _, width = kept.shape
    _, count, tokens, _ = weights.shape
    return pl.pallas_call(
        value_kernel,
        in_specs=[VMEM_SPEC] * 3,
        out_specs=[VMEM_SPEC] * count,
        out_shape=[jax.ShapeDtypeStruct((tokens, width), F32 if j == 0 else BF16) for j in range(count)],
        name="cross_values",
    )(weights, kept, come)


def final_kernel(scalar_ref, base_ref, temporal_ref, *refs):
    piece_refs, out_ref = refs[:-1], refs[-1]
    cols = piece_refs[0].shape[1]
    for j, piece_ref in enumerate(piece_refs):
        at = pl.ds(pl.multiple_of((scalar_ref[0] ^ j) * cols, HDIM), cols)
        total = base_ref[:, at] + temporal_ref[:, at].astype(F32)
        out_ref[:, at] = (total + piece_ref[...].astype(F32)).astype(BF16)


def final_sum(place, base, temporal, pieces):
    return pl.pallas_call(
        final_kernel,
        in_specs=[SMEM_SPEC] + [VMEM_SPEC] * (2 + len(pieces)),
        out_specs=VMEM_SPEC,
        out_shape=jax.ShapeDtypeStruct(base.shape, BF16),
        name="final",
    )(place.reshape(1), base, temporal, *pieces)


def temporal_plan(seq):
    if seq != 8:
        return [(k, k) for k in range(seq - 1, 0, -1)]
    return [(6, 2), (2, 6), (7, 3), (3, 7), (4, 4), (5, 5), (1, 1)]


def block(latent_qkv, cross_query, residual, prompt_states, kv_weight, prompt_lengths, assignment):
    tokens, width = cross_query.shape[2:]
    seq, grp, sides = (lax.axis_size(name) for name in ("seq", "grp", "hd"))
    me, group, side = (lax.axis_index(name) for name in ("seq", "grp", "hd"))
    core, near = me & 1, (me >> 1) & 1
    place = core * 2 + near
    feats = kv_weight.shape[0]
    _, rows_here, _ = prompt_states.shape
    rows_side = rows_here // sides
    rows = seq * rows_side

    parts = prompt_blocks(prompt_states, side, sides, seq)
    parts = lax.all_to_all(parts, "seq", 0, 0, tiled=True)

    qkv = latent_qkv[0, 0].transpose(1, 0, 2)
    share = tokens // seq
    steps = temporal_plan(seq)
    pieces, sources = [lax.dynamic_slice_in_dim(qkv, me * share, share, 1)], [me]
    held = qkv
    for number, (even, odd) in enumerate(steps):
        crossing = even & 1
        target = me ^ jnp.where(core == 0, even, odd)
        if number == 2:
            held, blocks = lax.optimization_barrier((qkv, blocks))
        block = lax.dynamic_slice_in_dim(held, target * share, share, 1)
        blocks = [block] if number == 0 else blocks + [block]
        sender_core = core ^ crossing
        sources.append(me ^ jnp.where(sender_core == 0, even, odd))
    for number, (even, odd) in enumerate(steps):
        pairs = [(i, i ^ (odd if i & 1 else even)) for i in range(seq)]
        pieces.append(lax.ppermute(blocks[number], "seq", pairs))

    half = width // 2
    planes = lax.optimization_barrier(kv_weight.transpose(1, 0, 2))
    mine = lax.dynamic_slice_in_dim(planes, core * half, half, 2)
    theirs = lax.dynamic_slice_in_dim(planes, (1 - core) * half, half, 2)
    come = swap(theirs, "seq", 1)
    across = [(g, s) for g in range(grp) for s in range(seq)]
    weights = []
    for kind in range(2):
        weights.append([mine[kind], come[kind]])
        for k in range(1, grp):
            for c, part in enumerate((mine[kind], theirs[kind])):
                pairs = [(g * seq + s, (g ^ k) * seq + (s ^ c)) for g, s in across]
                weights[kind].append(lax.ppermute(part, ("grp", "seq"), pairs))

    def slot(k):
        index = jnp.take(assignment, group ^ k)
        return lax.dynamic_index_in_dim(parts, index, 1, keepdims=False).reshape(rows, feats)

    wanted = jnp.stack([slot(0)] + [swap(slot(k), "grp", k) for k in range(1, grp)])
    n_pairs = [(s, h) for s in range(seq) for h in range(sides)]
    states = []
    for k in range(sides):
        for c in range(2):
            pairs = [(s * sides + h, (s ^ c) * sides + (h ^ k)) for s, h in n_pairs]
            states.append(wanted if k + c == 0 else lax.ppermute(wanted, ("seq", "hd"), pairs))

    quarter = width // 4
    query = cross_query[0, 0]
    queries = []
    for k, other in enumerate((0, 2, 1, 3)):
        block = lax.dynamic_slice_in_dim(query, (place ^ other) * quarter, quarter, 1)
        queries.append(block if k == 0 else swap(block, "seq", k))

    sums = []
    for kind in range(2):
        kept, sent = project(states, weights[kind], near)
        kept = kept + swap(sent, "seq", 2).astype(F32)
        bit = 4
        while bit < seq:
            come = swap(kept.astype(BF16), "seq", bit)
            bit *= 2
            if bit < seq:
                kept = kept + come.astype(F32)
        sums.append((kept, come))

    row = jnp.arange(rows * sides)
    which, source, inner = row // rows, (row % rows) // rows_side, row % rows_side
    position = source * rows_here + (which ^ side) * rows_side + inner
    length = jnp.take(prompt_lengths, jnp.take(assignment, group))
    bias = jnp.where(position < length, 0.0, -1e9).astype(F32)[None]

    base = spatial_attention(qkv, residual[0, 0])
    temporal = temporal_attention(jnp.stack(sources).astype(jnp.int32), pieces)
    temporal = lax.all_to_all(temporal, "seq", 0, 0, tiled=True).reshape(tokens, width)

    shares = cross_weights(bias, *sums[0], queries)
    crossed = cross_values(shares, *sums[1])
    results = [crossed[0]]
    for k in range(1, 4):
        results.append(swap(crossed[k], "seq", k))
    results[1], results[2] = results[2], results[1]
    return final_sum(place, base, temporal, results)[None, None]


def solution(mesh):
    return jax.shard_map(
        block,
        mesh=mesh,
        in_specs=(
            P("grp", "seq", None, None, "hd"),
            P("grp", "seq", None, "hd"),
            P("grp", "seq", None, "hd"),
            P(None, "seq", "grp"),
            P(("grp", "seq"), None, "hd"),
            P(),
            P(),
        ),
        out_specs=P("grp", "seq", None, "hd"),
        check_vma=False,
    )
```

```python
import functools
import math

import jax
import jax.numpy as jnp
from jax import lax
from jax.experimental import pallas as pl
from jax.experimental.pallas import tpu as pltpu
from jax.sharding import PartitionSpec as P


HDIM = 128
BF16 = jnp.bfloat16
F32 = jnp.float32


MODEST = pltpu.CompilerParams(vmem_limit_bytes=24 << 20)


def swap(value, axis, bits):
    pairs = [(i, i ^ bits) for i in range(lax.axis_size(axis))]
    return lax.ppermute(value, axis, pairs)


def scores_of(queries, key_rows):
    scores = lax.dot_general(queries, key_rows, (((1,), (1,)), ((), ())), preferred_element_type=F32)
    return scores * (1.0 / math.sqrt(HDIM))


def softmax(scores):
    powered = jnp.exp(scores - jnp.max(scores, axis=-1, keepdims=True))
    return (powered * (1.0 / jnp.sum(powered, axis=-1, keepdims=True))).astype(BF16)


def lanes(head):
    return slice(head * HDIM, (head + 1) * HDIM)


def block_cols(width, most=3):
    heads = width // HDIM
    return HDIM * max(n for n in range(1, most + 1) if heads % n == 0)


def prompt_kernel(scalar_ref, in_ref, out_ref):
    blocks, _, _, feats = out_ref.shape
    for j in range(blocks):
        out_ref[j] = in_ref[:, :, j * feats : (j + 1) * feats]


def prompt_blocks(states, side, sides, blocks):
    prompts, rows, width = states.shape
    rows, feats = rows // sides, width // blocks
    if feats % HDIM:
        cut = lax.dynamic_slice_in_dim(states, side * rows, rows, 1)
        return cut.reshape(prompts, rows, blocks, feats).transpose(2, 0, 1, 3)
    shape = (blocks, prompts, rows, feats)
    return pl.pallas_call(
        prompt_kernel,
        grid_spec=pltpu.PrefetchScalarGridSpec(
            num_scalar_prefetch=1,
            grid=(1,),
            in_specs=[pl.BlockSpec((prompts, rows, width), lambda j, s: (0, s[0], 0))],
            out_specs=pl.BlockSpec(shape, lambda j, s: (0, 0, 0, 0)),
        ),
        out_shape=jax.ShapeDtypeStruct(shape, BF16),
        compiler_params=MODEST,
        name="prompt_blocks",
    )(side.reshape(1), states)


def project_kernel(n_rows, scalar_ref, *refs):
    near = scalar_ref[0]
    state_refs = refs[: 2 * n_rows]
    kept_ref, sent_ref = refs[-2:]
    weight_refs = refs[2 * n_rows : -2]
    rows, cols = state_refs[0].shape[1], kept_ref.shape[1]

    def product(i, start):
        total = None
        for j, weight_ref in enumerate(weight_refs):
            state = state_refs[2 * i + j % 2][j // 2]
            weight = weight_ref[:, pl.ds(pl.multiple_of(start, HDIM), cols)]
            part = jnp.dot(state, weight, preferred_element_type=F32)
            total = part if total is None else total + part
        return total

    for i in range(n_rows):
        sent_ref[i * rows : (i + 1) * rows, :] = product(i, (1 - near) * cols).astype(BF16)
    for i in range(n_rows):
        kept_ref[i * rows : (i + 1) * rows, :] = product(i, near * cols)


VMEM_SPEC = pl.BlockSpec(memory_space=pltpu.VMEM)
SMEM_SPEC = pl.BlockSpec(memory_space=pltpu.SMEM)


def on_chip(*values):
    return [pltpu.with_memory_space_constraint(v, pltpu.VMEM) for v in values]


def project(states, weights, near):
    _, rows, _ = states[0].shape
    n_rows = len(states) // 2
    shape = (n_rows * rows, weights[0].shape[1] // 2)
    return pl.pallas_call(
        functools.partial(project_kernel, n_rows),
        in_specs=[SMEM_SPEC] + [VMEM_SPEC] * (len(states) + len(weights)),
        out_specs=[VMEM_SPEC] * 2,
        out_shape=[pltpu.VMEM(shape, F32), pltpu.VMEM(shape, BF16)],
        compiler_params=MODEST,
        name="project",
    )(near.reshape(1), *on_chip(*states, *weights))


def spatial_kernel(qkv_ref, residual_ref, out_ref):
    for head in range(out_ref.shape[1] // HDIM):
        at = lanes(head)
        weights = softmax(scores_of(qkv_ref[0, :, at], qkv_ref[1, :, at]))
        result = jnp.dot(weights, qkv_ref[2, :, at], preferred_element_type=F32)
        out_ref[:, at] = residual_ref[:, at].astype(F32) + result


def spatial_attention(qkv, residual):
    _, tokens, width = qkv.shape
    cols = block_cols(width)
    return pl.pallas_call(
        spatial_kernel,
        grid=(width // cols,),
        in_specs=[
            pl.BlockSpec((3, tokens, cols), lambda j: (0, 0, j)),
            pl.BlockSpec((tokens, cols), lambda j: (0, j)),
        ],
        out_specs=pl.BlockSpec((tokens, cols), lambda j: (0, j)),
        out_shape=jax.ShapeDtypeStruct((tokens, width), F32),
        compiler_params=MODEST,
        name="spatial",
    )(qkv, residual)


def temporal_kernel(frames, scalar_ref, *refs):
    frame_refs, out_ref = refs[:frames], refs[frames]
    _, tokens, cols = frame_refs[0].shape
    rows = frames * tokens
    row_token = lax.rem(lax.broadcasted_iota(jnp.int32, (rows, rows), 0), tokens)
    col_token = lax.rem(lax.broadcasted_iota(jnp.int32, (rows, rows), 1), tokens)
    same = row_token == col_token
    for head in range(cols // HDIM):
        at = lanes(head)
        query, key_rows, values = (
            jnp.concatenate([r[i, :, at] for r in frame_refs], axis=0) for i in range(3)
        )
        weights = softmax(jnp.where(same, scores_of(query, key_rows), -jnp.inf))
        result = jnp.dot(weights, values, preferred_element_type=F32).astype(BF16)
        for j in range(frames):
            out_ref[scalar_ref[j], :, at] = result[j * tokens : (j + 1) * tokens]


def temporal_attention(places, pieces):
    frames = len(pieces)
    _, tokens, width = pieces[0].shape
    cols = block_cols(width)
    return pl.pallas_call(
        functools.partial(temporal_kernel, frames),
        grid_spec=pltpu.PrefetchScalarGridSpec(
            num_scalar_prefetch=1,
            grid=(width // cols,),
            in_specs=[pl.BlockSpec((3, tokens, cols), lambda j, s: (0, 0, j))] * frames,
            out_specs=pl.BlockSpec((frames, tokens, cols), lambda j, s: (0, 0, j)),
        ),
        out_shape=jax.ShapeDtypeStruct((frames, tokens, width), BF16),
        compiler_params=MODEST,
        name="temporal",
    )(places, *pieces)


def weigh_kernel(bias_ref, kept_ref, come_ref, *refs):
    query_refs, out_ref = refs[:-1], refs[-1]
    for head in range(out_ref.shape[0]):
        at = lanes(head)
        key_rows = (kept_ref[:, at] + come_ref[:, at].astype(F32)).astype(BF16)
        for j, query_ref in enumerate(query_refs):
            out_ref[head, j] = softmax(scores_of(query_ref[:, at], key_rows) + bias_ref[...])


def cross_weights(bias, kept, come, queries):
    rows, width = kept.shape
    tokens = queries[0].shape[0]
    return pl.pallas_call(
        weigh_kernel,
        in_specs=[VMEM_SPEC] * (3 + len(queries)),
        out_specs=VMEM_SPEC,
        out_shape=pltpu.VMEM((width // HDIM, len(queries), tokens, rows), BF16),
        compiler_params=MODEST,
        name="cross_weights",
    )(*on_chip(bias, kept, come, *queries))


def value_kernel(weight_ref, kept_ref, come_ref, *out_refs):
    for head in range(weight_ref.shape[0]):
        at = lanes(head)
        values = (kept_ref[:, at] + come_ref[:, at].astype(F32)).astype(BF16)
        for j, out_ref in enumerate(out_refs):
            result = jnp.dot(weight_ref[head, j], values, preferred_element_type=F32)
            out_ref[:, at] = result.astype(out_ref.dtype)


def cross_values(weights, kept, come):
    _, width = kept.shape
    _, count, tokens, _ = weights.shape
    return pl.pallas_call(
        value_kernel,
        in_specs=[VMEM_SPEC] * 3,
        out_specs=[VMEM_SPEC] * count,
        out_shape=[pltpu.VMEM((tokens, width), F32 if j == 0 else BF16) for j in range(count)],
        compiler_params=MODEST,
        name="cross_values",
    )(*on_chip(weights, kept, come))


def final_kernel(scalar_ref, base_ref, temporal_ref, *refs):
    piece_refs, out_ref = refs[:-1], refs[-1]
    cols = piece_refs[0].shape[1]
    for j, piece_ref in enumerate(piece_refs):
        at = pl.ds(pl.multiple_of((scalar_ref[0] ^ j) * cols, HDIM), cols)
        total = base_ref[:, at] + temporal_ref[:, at].astype(F32)
        out_ref[:, at] = (total + piece_ref[...].astype(F32)).astype(BF16)


def final_sum(place, base, temporal, pieces):
    return pl.pallas_call(
        final_kernel,
        in_specs=[SMEM_SPEC] + [VMEM_SPEC] * (2 + len(pieces)),
        out_specs=VMEM_SPEC,
        out_shape=jax.ShapeDtypeStruct(base.shape, BF16),
        compiler_params=MODEST,
        name="final",
    )(place.reshape(1), *on_chip(base, temporal, *pieces))


def temporal_plan(seq):
    if seq != 8:
        return [(k, k) for k in range(seq - 1, 0, -1)]
    return [(6, 2), (2, 6), (7, 3), (3, 7), (4, 4), (5, 5), (1, 1)]


def block(latent_qkv, cross_query, residual, prompt_states, kv_weight, prompt_lengths, assignment):
    tokens, width = cross_query.shape[2:]
    seq, grp, sides = (lax.axis_size(name) for name in ("seq", "grp", "hd"))
    me, group, side = (lax.axis_index(name) for name in ("seq", "grp", "hd"))
    core, near = me & 1, (me >> 1) & 1
    place = core * 2 + near
    feats = kv_weight.shape[0]
    _, rows_here, _ = prompt_states.shape
    rows_side = rows_here // sides
    rows = seq * rows_side

    parts = prompt_blocks(prompt_states, side, sides, seq)
    parts = lax.all_to_all(parts, "seq", 0, 0, tiled=True)

    qkv = latent_qkv[0, 0].transpose(1, 0, 2)
    share = tokens // seq
    steps = temporal_plan(seq)
    pieces, sources = [lax.dynamic_slice_in_dim(qkv, me * share, share, 1)], [me]
    held = qkv
    for number, (even, odd) in enumerate(steps):
        crossing = even & 1
        target = me ^ jnp.where(core == 0, even, odd)
        if number == 2:
            held, blocks = lax.optimization_barrier((qkv, blocks))
        block = lax.dynamic_slice_in_dim(held, target * share, share, 1)
        blocks = [block] if number == 0 else blocks + [block]
        sender_core = core ^ crossing
        sources.append(me ^ jnp.where(sender_core == 0, even, odd))
    for number, (even, odd) in enumerate(steps):
        pairs = [(i, i ^ (odd if i & 1 else even)) for i in range(seq)]
        pieces.append(lax.ppermute(blocks[number], "seq", pairs))

    half = width // 2
    planes = lax.optimization_barrier(kv_weight.transpose(1, 0, 2))
    mine = lax.dynamic_slice_in_dim(planes, core * half, half, 2)
    theirs = lax.dynamic_slice_in_dim(planes, (1 - core) * half, half, 2)
    come = swap(theirs, "seq", 1)
    across = [(g, s) for g in range(grp) for s in range(seq)]
    weights = []
    for kind in range(2):
        weights.append([mine[kind], come[kind]])
        for k in range(1, grp):
            for c, part in enumerate((mine[kind], theirs[kind])):
                pairs = [(g * seq + s, (g ^ k) * seq + (s ^ c)) for g, s in across]
                weights[kind].append(lax.ppermute(part, ("grp", "seq"), pairs))

    def slot(k):
        index = lax.dynamic_index_in_dim(assignment, group ^ k, keepdims=False)
        return lax.dynamic_index_in_dim(parts, index, 1, keepdims=False).reshape(rows, feats)

    wanted = jnp.stack([slot(0)] + [swap(slot(k), "grp", k) for k in range(1, grp)])
    states = []
    for k in range(sides):
        if k:
            other = swap(wanted, "hd", k)
        else:
            other = wanted
        states += [other, swap(other, "seq", 1)]

    quarter = width // 4
    query = cross_query[0, 0]
    queries = []
    for k, other in enumerate((0, 2, 1, 3)):
        block = lax.dynamic_slice_in_dim(query, (place ^ other) * quarter, quarter, 1)
        queries.append(block if k == 0 else swap(block, "seq", k))

    sums = []
    for kind in range(2):
        kept, sent = project(states, weights[kind], near)
        kept = kept + swap(sent, "seq", 2).astype(F32)
        bit = 4
        while bit < seq:
            come = swap(kept.astype(BF16), "seq", bit)
            bit *= 2
            if bit < seq:
                kept = kept + come.astype(F32)
        sums.append((kept, come))

    row = jnp.arange(rows * sides)
    which, source, inner = row // rows, (row % rows) // rows_side, row % rows_side
    position = source * rows_here + (which ^ side) * rows_side + inner
    served = lax.dynamic_index_in_dim(assignment, group, keepdims=False)
    length = lax.dynamic_index_in_dim(prompt_lengths, served, keepdims=False)
    bias = jnp.where(position < length, 0.0, -1e9).astype(F32)[None]

    base = spatial_attention(qkv, residual[0, 0])
    temporal = temporal_attention(jnp.stack(sources).astype(jnp.int32), pieces)
    temporal = lax.all_to_all(temporal, "seq", 0, 0, tiled=True).reshape(tokens, width)

    shares = cross_weights(bias, *sums[0], queries)
    crossed = cross_values(shares, *sums[1])
    results = [crossed[0]]
    for k in range(1, 4):
        results.append(swap(crossed[k], "seq", k))
    results[1], results[2] = results[2], results[1]
    return final_sum(place, base, temporal, results)[None, None]


def solution(mesh):
    return jax.shard_map(
        block,
        mesh=mesh,
        in_specs=(
            P("grp", "seq", None, None, "hd"),
            P("grp", "seq", None, "hd"),
            P("grp", "seq", None, "hd"),
            P(None, "seq", "grp"),
            P(("grp", "seq"), None, "hd"),
            P(),
            P(),
        ),
        out_specs=P("grp", "seq", None, "hd"),
        check_vma=False,
    )
```

```python
import functools
import math

import jax
import jax.numpy as jnp
from jax import lax
from jax.experimental import pallas as pl
from jax.experimental.pallas import tpu as pltpu
from jax.sharding import PartitionSpec as P


HDIM = 128
BF16 = jnp.bfloat16
F32 = jnp.float32


MODEST = pltpu.CompilerParams(vmem_limit_bytes=24 << 20)

VMEM_SPEC = pl.BlockSpec(memory_space=pltpu.VMEM)
SMEM_SPEC = pl.BlockSpec(memory_space=pltpu.SMEM)


def on_chip(*values):
    return [pltpu.with_memory_space_constraint(v, pltpu.VMEM) for v in values]


def swap(value, axis, bits):
    pairs = [(i, i ^ bits) for i in range(lax.axis_size(axis))]
    return lax.ppermute(value, axis, pairs)


def scores_of(queries, key_rows):
    scores = lax.dot_general(queries, key_rows, (((1,), (1,)), ((), ())), preferred_element_type=F32)
    return scores * (1.0 / math.sqrt(HDIM))


def softmax(scores):
    powered = jnp.exp(scores - jnp.max(scores, axis=-1, keepdims=True))
    return (powered * (1.0 / jnp.sum(powered, axis=-1, keepdims=True))).astype(BF16)


def lanes(head):
    return slice(head * HDIM, (head + 1) * HDIM)


def block_cols(width, most=3):
    heads = width // HDIM
    return HDIM * max(n for n in range(1, most + 1) if heads % n == 0)


def prompt_kernel(scalar_ref, in_ref, out_ref):
    blocks, _, _, feats = out_ref.shape
    for j in range(blocks):
        out_ref[j] = in_ref[:, :, j * feats : (j + 1) * feats]


def prompt_blocks(states, side, sides, blocks):
    prompts, rows, width = states.shape
    rows, feats = rows // sides, width // blocks
    if feats % HDIM:
        cut = lax.dynamic_slice_in_dim(states, side * rows, rows, 1)
        return cut.reshape(prompts, rows, blocks, feats).transpose(2, 0, 1, 3)
    shape = (blocks, prompts, rows, feats)
    return pl.pallas_call(
        prompt_kernel,
        grid_spec=pltpu.PrefetchScalarGridSpec(
            num_scalar_prefetch=1,
            grid=(1,),
            in_specs=[pl.BlockSpec((prompts, rows, width), lambda j, s: (0, s[0], 0))],
            out_specs=pl.BlockSpec(shape, lambda j, s: (0, 0, 0, 0)),
        ),
        out_shape=jax.ShapeDtypeStruct(shape, BF16),
        compiler_params=MODEST,
        name="prompt_blocks",
    )(side.reshape(1), states)


def pick_kernel(assignment_ref, group_ref, parts_ref, *out_refs):
    blocks, _, rows, _ = parts_ref.shape
    for k, out_ref in enumerate(out_refs):
        slot = assignment_ref[group_ref[0] ^ k]
        for j in range(blocks):
            out_ref[j * rows : (j + 1) * rows, :] = parts_ref[j, slot]


def pick_slots(assignment, group, parts, n_grp):
    blocks, _, rows, feats = parts.shape
    if feats % HDIM:
        slots = [lax.dynamic_index_in_dim(assignment, group ^ k, keepdims=False) for k in range(n_grp)]
        cut = [lax.dynamic_index_in_dim(parts, slot, 1, keepdims=False) for slot in slots]
        return [c.reshape(blocks * rows, feats) for c in cut]
    return pl.pallas_call(
        pick_kernel,
        in_specs=[SMEM_SPEC, SMEM_SPEC, VMEM_SPEC],
        out_specs=[VMEM_SPEC] * n_grp,
        out_shape=[pltpu.VMEM((blocks * rows, feats), BF16)] * n_grp,
        compiler_params=MODEST,
        name="pick_slots",
    )(assignment, group.reshape(1), *on_chip(parts))


def project_kernel(n_rows, scalar_ref, *refs):
    near = scalar_ref[0]
    state_refs = refs[: 2 * n_rows]
    kept_ref, sent_ref = refs[-2:]
    weight_refs = refs[2 * n_rows : -2]
    rows, cols = state_refs[0].shape[1], kept_ref.shape[1]

    def product(i, start):
        total = None
        for j, weight_ref in enumerate(weight_refs):
            state = state_refs[2 * i + j % 2][j // 2]
            weight = weight_ref[:, pl.ds(pl.multiple_of(start, HDIM), cols)]
            part = jnp.dot(state, weight, preferred_element_type=F32)
            total = part if total is None else total + part
        return total

    for i in range(n_rows):
        sent_ref[i * rows : (i + 1) * rows, :] = product(i, (1 - near) * cols).astype(BF16)
    for i in range(n_rows):
        kept_ref[i * rows : (i + 1) * rows, :] = product(i, near * cols)


def project(states, weights, near):
    _, rows, _ = states[0].shape
    n_rows = len(states) // 2
    shape = (n_rows * rows, weights[0].shape[1] // 2)
    return pl.pallas_call(
        functools.partial(project_kernel, n_rows),
        in_specs=[SMEM_SPEC] + [VMEM_SPEC] * (len(states) + len(weights)),
        out_specs=[VMEM_SPEC] * 2,
        out_shape=[jax.ShapeDtypeStruct(shape, F32), pltpu.VMEM(shape, BF16)],
        compiler_params=MODEST,
        name="project",
    )(near.reshape(1), *states, *weights[:2], *on_chip(*weights[2:]))


def spatial_kernel(qkv_ref, residual_ref, out_ref):
    for head in range(out_ref.shape[1] // HDIM):
        at = lanes(head)
        weights = softmax(scores_of(qkv_ref[0, :, at], qkv_ref[1, :, at]))
        result = jnp.dot(weights, qkv_ref[2, :, at], preferred_element_type=F32)
        out_ref[:, at] = residual_ref[:, at].astype(F32) + result


def spatial_attention(qkv, residual):
    _, tokens, width = qkv.shape
    cols = block_cols(width)
    return pl.pallas_call(
        spatial_kernel,
        grid=(width // cols,),
        in_specs=[
            pl.BlockSpec((3, tokens, cols), lambda j: (0, 0, j)),
            pl.BlockSpec((tokens, cols), lambda j: (0, j)),
        ],
        out_specs=pl.BlockSpec((tokens, cols), lambda j: (0, j)),
        out_shape=pltpu.HBM((tokens, width), F32),
        compiler_params=MODEST,
        name="spatial",
    )(qkv, residual)


def temporal_kernel(frames, scalar_ref, *refs):
    frame_refs, out_ref = refs[:frames], refs[frames]
    _, tokens, cols = frame_refs[0].shape
    rows = frames * tokens
    row_token = lax.rem(lax.broadcasted_iota(jnp.int32, (rows, rows), 0), tokens)
    col_token = lax.rem(lax.broadcasted_iota(jnp.int32, (rows, rows), 1), tokens)
    same = row_token == col_token
    for head in range(cols // HDIM):
        at = lanes(head)
        query, key_rows, values = (
            jnp.concatenate([r[i, :, at] for r in frame_refs], axis=0) for i in range(3)
        )
        weights = softmax(jnp.where(same, scores_of(query, key_rows), -jnp.inf))
        result = jnp.dot(weights, values, preferred_element_type=F32).astype(BF16)
        for j in range(frames):
            out_ref[scalar_ref[j], :, at] = result[j * tokens : (j + 1) * tokens]


def temporal_attention(places, pieces):
    frames = len(pieces)
    _, tokens, width = pieces[0].shape
    cols = block_cols(width)
    return pl.pallas_call(
        functools.partial(temporal_kernel, frames),
        grid_spec=pltpu.PrefetchScalarGridSpec(
            num_scalar_prefetch=1,
            grid=(width // cols,),
            in_specs=[pl.BlockSpec((3, tokens, cols), lambda j, s: (0, 0, j))] * frames,
            out_specs=pl.BlockSpec((frames, tokens, cols), lambda j, s: (0, 0, j)),
        ),
        out_shape=jax.ShapeDtypeStruct((frames, tokens, width), BF16),
        compiler_params=MODEST,
        name="temporal",
    )(places, *pieces)


def weigh_kernel(bias_ref, kept_ref, come_ref, *refs):
    query_refs, out_ref = refs[:-1], refs[-1]
    for head in range(out_ref.shape[0]):
        at = lanes(head)
        key_rows = (kept_ref[:, at] + come_ref[:, at].astype(F32)).astype(BF16)
        for j, query_ref in enumerate(query_refs):
            out_ref[head, j] = softmax(scores_of(query_ref[:, at], key_rows) + bias_ref[...])


def cross_weights(bias, kept, come, queries):
    rows, width = kept.shape
    tokens = queries[0].shape[0]
    return pl.pallas_call(
        weigh_kernel,
        in_specs=[VMEM_SPEC] * (3 + len(queries)),
        out_specs=VMEM_SPEC,
        out_shape=pltpu.VMEM((width // HDIM, len(queries), tokens, rows), BF16),
        compiler_params=MODEST,
        name="cross_weights",
    )(bias, kept, *on_chip(come), *queries)


def value_kernel(weight_ref, kept_ref, come_ref, *out_refs):
    for head in range(weight_ref.shape[0]):
        at = lanes(head)
        values = (kept_ref[:, at] + come_ref[:, at].astype(F32)).astype(BF16)
        for j, out_ref in enumerate(out_refs):
            result = jnp.dot(weight_ref[head, j], values, preferred_element_type=F32)
            out_ref[:, at] = result.astype(out_ref.dtype)


def cross_values(weights, kept, come):
    _, width = kept.shape
    _, count, tokens, _ = weights.shape
    return pl.pallas_call(
        value_kernel,
        in_specs=[VMEM_SPEC] * 3,
        out_specs=[VMEM_SPEC] * count,
        out_shape=[pltpu.VMEM((tokens, width), F32)]
        + [pltpu.VMEM((tokens, width), BF16)] * (count - 1),
        compiler_params=MODEST,
        name="cross_values",
    )(*on_chip(weights), kept, *on_chip(come))


def gather_kernel(scalar_ref, base_ref, *refs):
    piece_refs, out_ref = refs[:-1], refs[-1]
    for j, piece_ref in enumerate(piece_refs):

        @pl.when(pl.program_id(0) == j)
        def _(piece_ref=piece_ref):
            out_ref[...] = base_ref[...] + piece_ref[...].astype(F32)


def gather_results(place, base, pieces):
    tokens, width = base.shape
    cols = width // len(pieces)
    side = pl.BlockSpec((tokens, cols), lambda j, s: (0, j ^ s[0]))
    return pl.pallas_call(
        gather_kernel,
        grid_spec=pltpu.PrefetchScalarGridSpec(
            num_scalar_prefetch=1,
            grid=(len(pieces),),
            in_specs=[side] + [VMEM_SPEC] * len(pieces),
            out_specs=side,
        ),
        out_shape=jax.ShapeDtypeStruct(base.shape, F32),
        compiler_params=MODEST,
        name="gather_results",
    )(place.reshape(1), base, *on_chip(*pieces))


def temporal_plan(seq):
    if seq != 8:
        return [(k, k) for k in range(seq - 1, 0, -1)]
    return [(6, 2), (2, 6), (7, 3), (3, 7), (4, 4), (5, 5), (1, 1)]


def block(latent_qkv, cross_query, residual, prompt_states, kv_weight, prompt_lengths, assignment):
    tokens, width = cross_query.shape[2:]
    seq, grp, sides = (lax.axis_size(name) for name in ("seq", "grp", "hd"))
    me, group, side = (lax.axis_index(name) for name in ("seq", "grp", "hd"))
    core, near = me & 1, (me >> 1) & 1
    place = core * 2 + near
    feats = kv_weight.shape[0]
    _, rows_here, _ = prompt_states.shape
    rows_side = rows_here // sides
    rows = seq * rows_side

    parts = prompt_blocks(prompt_states, side, sides, seq)
    parts = lax.all_to_all(parts, "seq", 0, 0, tiled=True)

    qkv = latent_qkv[0, 0].transpose(1, 0, 2)
    share = tokens // seq
    steps = temporal_plan(seq)
    pieces, sources = [lax.dynamic_slice_in_dim(qkv, me * share, share, 1)], [me]
    held = qkv
    for number, (even, odd) in enumerate(steps):
        crossing = even & 1
        target = me ^ jnp.where(core == 0, even, odd)
        if number == 2:
            held, blocks = lax.optimization_barrier((qkv, blocks))
        block = lax.dynamic_slice_in_dim(held, target * share, share, 1)
        blocks = [block] if number == 0 else blocks + [block]
        sender_core = core ^ crossing
        sources.append(me ^ jnp.where(sender_core == 0, even, odd))
    for number, (even, odd) in enumerate(steps):
        pairs = [(i, i ^ (odd if i & 1 else even)) for i in range(seq)]
        pieces.append(lax.ppermute(blocks[number], "seq", pairs))

    half = width // 2
    planes = lax.optimization_barrier(kv_weight.transpose(1, 0, 2))
    across = [(g, q) for g in range(grp) for q in range(seq)]

    def halves(source, kind):
        cut = (lax.dynamic_slice(source, (kind, 0, c * half), (1, feats, half)) for c in (core, 1 - core))
        return tuple(c.reshape(feats, half) for c in cut)

    keys = halves(planes, 0)
    later, keys = lax.optimization_barrier((planes, keys))
    weights = [keys, halves(later, 1)]
    for kind in range(2):
        mine, theirs = weights[kind]
        weights[kind] = [mine, swap(theirs, "seq", 1)]
        for k in range(1, grp):
            for c, part in enumerate((mine, theirs)):
                pairs = [(g * seq + q, (g ^ k) * seq + (q ^ c)) for g, q in across]
                weights[kind].append(lax.ppermute(part, ("grp", "seq"), pairs))

    slots = pick_slots(assignment, group, parts, grp)
    wanted = jnp.stack([slots[0]] + [swap(slots[k], "grp", k) for k in range(1, grp)])
    states = []
    for k in range(sides):
        if k:
            other = swap(wanted, "hd", k)
        else:
            other = wanted
        states += [other, swap(other, "seq", 1)]

    quarter = width // 4
    query = cross_query[0, 0]
    queries = []
    for k, other in enumerate((0, 2, 1, 3)):
        block = lax.dynamic_slice_in_dim(query, (place ^ other) * quarter, quarter, 1)
        queries.append(block if k == 0 else swap(block, "seq", k))

    sums = []
    for kind in range(2):
        kept, sent = project(states, weights[kind], near)
        kept = kept + swap(sent, "seq", 2).astype(F32)
        bit = 4
        while bit < seq:
            come = swap(kept.astype(BF16), "seq", bit)
            bit *= 2
            if bit < seq:
                kept = kept + come.astype(F32)
        sums.append((kept, come))

    row = jnp.arange(rows * sides)
    which, source, inner = row // rows, (row % rows) // rows_side, row % rows_side
    position = source * rows_here + (which ^ side) * rows_side + inner
    served = lax.dynamic_index_in_dim(assignment, group, keepdims=False)
    length = lax.dynamic_index_in_dim(prompt_lengths, served, keepdims=False)
    bias = jnp.where(position < length, 0.0, -1e9).astype(F32)[None]

    base = spatial_attention(qkv, residual[0, 0])
    temporal = temporal_attention(jnp.stack(sources).astype(jnp.int32), pieces)
    temporal = lax.all_to_all(temporal, "seq", 0, 0, tiled=True).reshape(tokens, width)

    shares = cross_weights(bias, *sums[0], queries)
    crossed = cross_values(shares, *sums[1])
    results = [crossed[0]]
    for k in range(1, 4):
        results.append(swap(crossed[k], "seq", k))
    results[1], results[2] = results[2], results[1]
    total = gather_results(place, base, results)
    return (total + temporal.astype(F32)).astype(BF16)[None, None]


def solution(mesh):
    return jax.shard_map(
        block,
        mesh=mesh,
        in_specs=(
            P("grp", "seq", None, None, "hd"),
            P("grp", "seq", None, "hd"),
            P("grp", "seq", None, "hd"),
            P(None, "seq", "grp"),
            P(("grp", "seq"), None, "hd"),
            P(),
            P(),
        ),
        out_specs=P("grp", "seq", None, "hd"),
        check_vma=False,
    )
```

```python
import functools
import math

import jax
import jax.numpy as jnp
from jax import lax
from jax.experimental import pallas as pl
from jax.experimental.pallas import tpu as pltpu
from jax.sharding import PartitionSpec as P


HDIM = 128
BF16 = jnp.bfloat16
F32 = jnp.float32


MODEST = pltpu.CompilerParams(vmem_limit_bytes=24 << 20)

VMEM_SPEC = pl.BlockSpec(memory_space=pltpu.VMEM)
SMEM_SPEC = pl.BlockSpec(memory_space=pltpu.SMEM)


def on_chip(*values):
    return [pltpu.with_memory_space_constraint(v, pltpu.VMEM) for v in values]


def swap(value, axis, bits):
    pairs = [(i, i ^ bits) for i in range(lax.axis_size(axis))]
    return lax.ppermute(value, axis, pairs)


def scores_of(queries, key_rows):
    scores = lax.dot_general(queries, key_rows, (((1,), (1,)), ((), ())), preferred_element_type=F32)
    return scores * (1.0 / math.sqrt(HDIM))


def softmax(scores):
    powered = jnp.exp(scores - jnp.max(scores, axis=-1, keepdims=True))
    return (powered * (1.0 / jnp.sum(powered, axis=-1, keepdims=True))).astype(BF16)


def lanes(head):
    return slice(head * HDIM, (head + 1) * HDIM)


def block_cols(width, most=3):
    heads = width // HDIM
    return HDIM * max(n for n in range(1, most + 1) if heads % n == 0)


def prompt_kernel(scalar_ref, in_ref, out_ref):
    blocks, _, _, feats = out_ref.shape
    for j in range(blocks):
        out_ref[j] = in_ref[:, :, j * feats : (j + 1) * feats]


def prompt_blocks(states, side, sides, blocks):
    prompts, rows, width = states.shape
    rows, feats = rows // sides, width // blocks
    if feats % HDIM:
        cut = lax.dynamic_slice_in_dim(states, side * rows, rows, 1)
        return cut.reshape(prompts, rows, blocks, feats).transpose(2, 0, 1, 3)
    shape = (blocks, prompts, rows, feats)
    return pl.pallas_call(
        prompt_kernel,
        grid_spec=pltpu.PrefetchScalarGridSpec(
            num_scalar_prefetch=1,
            grid=(1,),
            in_specs=[pl.BlockSpec((prompts, rows, width), lambda j, s: (0, s[0], 0))],
            out_specs=pl.BlockSpec(shape, lambda j, s: (0, 0, 0, 0)),
        ),
        out_shape=jax.ShapeDtypeStruct(shape, BF16),
        compiler_params=MODEST,
        name="prompt_blocks",
    )(side.reshape(1), states)


def pick_kernel(assignment_ref, group_ref, parts_ref, *out_refs):
    blocks, _, rows, _ = parts_ref.shape
    for k, out_ref in enumerate(out_refs):
        slot = assignment_ref[group_ref[0] ^ k]
        for j in range(blocks):
            out_ref[j * rows : (j + 1) * rows, :] = parts_ref[j, slot]


def pick_slots(assignment, group, parts, n_grp):
    blocks, _, rows, feats = parts.shape
    if feats % HDIM:
        slots = [lax.dynamic_index_in_dim(assignment, group ^ k, keepdims=False) for k in range(n_grp)]
        cut = [lax.dynamic_index_in_dim(parts, slot, 1, keepdims=False) for slot in slots]
        return [c.reshape(blocks * rows, feats) for c in cut]
    return pl.pallas_call(
        pick_kernel,
        in_specs=[SMEM_SPEC, SMEM_SPEC, VMEM_SPEC],
        out_specs=[VMEM_SPEC] * n_grp,
        out_shape=[pltpu.VMEM((blocks * rows, feats), BF16)] * n_grp,
        compiler_params=MODEST,
        name="pick_slots",
    )(assignment, group.reshape(1), *on_chip(parts))


def project_kernel(n_rows, scalar_ref, *refs):
    near = scalar_ref[0]
    state_refs = refs[: 2 * n_rows]
    kept_ref, sent_ref = refs[-2:]
    weight_refs = refs[2 * n_rows : -2]
    rows, cols = state_refs[0].shape[1], kept_ref.shape[1]

    def product(i, start):
        total = None
        for j, weight_ref in enumerate(weight_refs):
            state = state_refs[2 * i + j % 2][j // 2]
            weight = weight_ref[:, pl.ds(pl.multiple_of(start, HDIM), cols)]
            part = jnp.dot(state, weight, preferred_element_type=F32)
            total = part if total is None else total + part
        return total

    for i in range(n_rows):
        sent_ref[i * rows : (i + 1) * rows, :] = product(i, (1 - near) * cols).astype(BF16)
    for i in range(n_rows):
        kept_ref[i * rows : (i + 1) * rows, :] = product(i, near * cols)


def project(states, weights, near):
    _, rows, _ = states[0].shape
    n_rows = len(states) // 2
    shape = (n_rows * rows, weights[0].shape[1] // 2)
    return pl.pallas_call(
        functools.partial(project_kernel, n_rows),
        in_specs=[SMEM_SPEC] + [VMEM_SPEC] * (len(states) + len(weights)),
        out_specs=[VMEM_SPEC] * 2,
        out_shape=[jax.ShapeDtypeStruct(shape, F32), pltpu.VMEM(shape, BF16)],
        compiler_params=MODEST,
        name="project",
    )(near.reshape(1), *states, *weights[:2], *on_chip(*weights[2:]))


def spatial_kernel(qkv_ref, residual_ref, out_ref):
    for head in range(out_ref.shape[1] // HDIM):
        at = lanes(head)
        weights = softmax(scores_of(qkv_ref[0, :, at], qkv_ref[1, :, at]))
        result = jnp.dot(weights, qkv_ref[2, :, at], preferred_element_type=F32)
        out_ref[:, at] = residual_ref[:, at].astype(F32) + result


def spatial_attention(qkv, residual):
    _, tokens, width = qkv.shape
    cols = block_cols(width)
    return pl.pallas_call(
        spatial_kernel,
        grid=(width // cols,),
        in_specs=[
            pl.BlockSpec((3, tokens, cols), lambda j: (0, 0, j)),
            pl.BlockSpec((tokens, cols), lambda j: (0, j)),
        ],
        out_specs=pl.BlockSpec((tokens, cols), lambda j: (0, j)),
        out_shape=pltpu.HBM((tokens, width), F32),
        compiler_params=MODEST,
        name="spatial",
    )(qkv, residual)


def temporal_kernel(plan, scalar_ref, *refs):
    frames = len(plan[0])
    frame_refs, out_refs = refs[:frames], refs[frames:]
    _, tokens, cols = frame_refs[0].shape
    rows = frames * tokens
    row_token = lax.rem(lax.broadcasted_iota(jnp.int32, (rows, rows), 0), tokens)
    col_token = lax.rem(lax.broadcasted_iota(jnp.int32, (rows, rows), 1), tokens)
    same = row_token == col_token
    even = scalar_ref[0] == 0
    for head in range(cols // HDIM):
        at = lanes(head)
        query, key_rows, values = (
            jnp.concatenate([r[i, :, at] for r in frame_refs], axis=0) for i in range(3)
        )
        weights = softmax(jnp.where(same, scores_of(query, key_rows), -jnp.inf))
        result = jnp.dot(weights, values, preferred_element_type=F32)
        parts = [result[j * tokens : (j + 1) * tokens] for j in range(frames)]
        for out_ref, first, second in zip(out_refs, *plan):
            part = parts[first] if first == second else jnp.where(even, parts[first], parts[second])
            out_ref[:, at] = part.astype(BF16)


def temporal_attention(core, plan, pieces):
    _, tokens, width = pieces[0].shape
    cols = block_cols(width)
    return pl.pallas_call(
        functools.partial(temporal_kernel, plan),
        grid_spec=pltpu.PrefetchScalarGridSpec(
            num_scalar_prefetch=1,
            grid=(width // cols,),
            in_specs=[pl.BlockSpec((3, tokens, cols), lambda j, s: (0, 0, j))] * len(pieces),
            out_specs=[pl.BlockSpec((tokens, cols), lambda j, s: (0, j))] * len(pieces),
        ),
        out_shape=[jax.ShapeDtypeStruct((tokens, width), BF16)] * len(pieces),
        compiler_params=MODEST,
        name="temporal",
    )(core.reshape(1), *pieces)


def weigh_kernel(bias_ref, kept_ref, come_ref, *refs):
    query_refs, out_ref = refs[:-1], refs[-1]
    for head in range(out_ref.shape[0]):
        at = lanes(head)
        key_rows = (kept_ref[:, at] + come_ref[:, at].astype(F32)).astype(BF16)
        for j, query_ref in enumerate(query_refs):
            out_ref[head, j] = softmax(scores_of(query_ref[:, at], key_rows) + bias_ref[...])


def cross_weights(bias, kept, come, queries):
    rows, width = kept.shape
    tokens = queries[0].shape[0]
    return pl.pallas_call(
        weigh_kernel,
        in_specs=[VMEM_SPEC] * (3 + len(queries)),
        out_specs=VMEM_SPEC,
        out_shape=pltpu.VMEM((width // HDIM, len(queries), tokens, rows), BF16),
        compiler_params=MODEST,
        name="cross_weights",
    )(bias, kept, *on_chip(come), *queries)


def value_kernel(weight_ref, kept_ref, come_ref, *out_refs):
    for head in range(weight_ref.shape[0]):
        at = lanes(head)
        values = (kept_ref[:, at] + come_ref[:, at].astype(F32)).astype(BF16)
        for j, out_ref in enumerate(out_refs):
            result = jnp.dot(weight_ref[head, j], values, preferred_element_type=F32)
            out_ref[:, at] = result.astype(out_ref.dtype)


def cross_values(weights, kept, come):
    _, width = kept.shape
    _, count, tokens, _ = weights.shape
    return pl.pallas_call(
        value_kernel,
        in_specs=[VMEM_SPEC] * 3,
        out_specs=[VMEM_SPEC] * count,
        out_shape=[pltpu.VMEM((tokens, width), F32)]
        + [pltpu.VMEM((tokens, width), BF16)] * (count - 1),
        compiler_params=MODEST,
        name="cross_values",
    )(*on_chip(weights), kept, *on_chip(come))


def gather_kernel(scalar_ref, base_ref, *refs):
    piece_refs, out_ref = refs[:-1], refs[-1]
    for j, piece_ref in enumerate(piece_refs):

        @pl.when(pl.program_id(0) == j)
        def _(piece_ref=piece_ref):
            out_ref[...] = base_ref[...] + piece_ref[...].astype(F32)


def gather_results(place, base, pieces):
    tokens, width = base.shape
    cols = width // len(pieces)
    side = pl.BlockSpec((tokens, cols), lambda j, s: (0, j ^ s[0]))
    return pl.pallas_call(
        gather_kernel,
        grid_spec=pltpu.PrefetchScalarGridSpec(
            num_scalar_prefetch=1,
            grid=(len(pieces),),
            in_specs=[side] + [VMEM_SPEC] * len(pieces),
            out_specs=side,
        ),
        out_shape=pltpu.VMEM(base.shape, F32),
        compiler_params=MODEST,
        name="gather_results",
    )(place.reshape(1), base, *on_chip(*pieces))


def final_kernel(scalar_ref, total_ref, *refs):
    piece_refs, out_ref = refs[:-1], refs[-1]
    rows = piece_refs[0].shape[0]
    for k, piece_ref in enumerate(piece_refs):
        at = pl.ds(pl.multiple_of((scalar_ref[0] ^ k) * rows, rows), rows)
        out_ref[at, :] = (total_ref[at, :] + piece_ref[...].astype(F32)).astype(BF16)


def final_sum(me, total, pieces):
    return pl.pallas_call(
        final_kernel,
        in_specs=[SMEM_SPEC] + [VMEM_SPEC] * (1 + len(pieces)),
        out_specs=VMEM_SPEC,
        out_shape=jax.ShapeDtypeStruct(total.shape, BF16),
        compiler_params=MODEST,
        name="final",
    )(me.reshape(1), *on_chip(total, *pieces))


def temporal_plan(seq):
    if seq != 8:
        return [(k, k) for k in range(seq - 1, 0, -1)]
    return [(6, 2), (2, 6), (7, 3), (3, 7), (4, 4), (5, 5), (1, 1)]


def block(latent_qkv, cross_query, residual, prompt_states, kv_weight, prompt_lengths, assignment):
    tokens, width = cross_query.shape[2:]
    seq, grp, sides = (lax.axis_size(name) for name in ("seq", "grp", "hd"))
    me, group, side = (lax.axis_index(name) for name in ("seq", "grp", "hd"))
    core, near = me & 1, (me >> 1) & 1
    place = core * 2 + near
    feats = kv_weight.shape[0]
    _, rows_here, _ = prompt_states.shape
    rows_side = rows_here // sides
    rows = seq * rows_side

    parts = prompt_blocks(prompt_states, side, sides, seq)
    parts = lax.all_to_all(parts, "seq", 0, 0, tiled=True)

    qkv = latent_qkv[0, 0].transpose(1, 0, 2)
    share = tokens // seq
    steps = temporal_plan(seq)
    pieces = [lax.dynamic_slice_in_dim(qkv, me * share, share, 1)]
    held = qkv
    for number, (even, odd) in enumerate(steps):
        target = me ^ jnp.where(core == 0, even, odd)
        if number == 2:
            held, blocks = lax.optimization_barrier((qkv, blocks))
        block = lax.dynamic_slice_in_dim(held, target * share, share, 1)
        blocks = [block] if number == 0 else blocks + [block]
    for number, (even, odd) in enumerate(steps):
        pairs = [(i, i ^ (odd if i & 1 else even)) for i in range(seq)]
        pieces.append(lax.ppermute(blocks[number], "seq", pairs))

    half = width // 2
    planes = lax.optimization_barrier(kv_weight.transpose(1, 0, 2))
    across = [(g, q) for g in range(grp) for q in range(seq)]

    def halves(source, kind):
        cut = (lax.dynamic_slice(source, (kind, 0, c * half), (1, feats, half)) for c in (core, 1 - core))
        return tuple(c.reshape(feats, half) for c in cut)

    keys = halves(planes, 0)
    later, keys = lax.optimization_barrier((planes, keys))
    weights = [keys, halves(later, 1)]
    for kind in range(2):
        mine, theirs = weights[kind]
        weights[kind] = [mine, swap(theirs, "seq", 1)]
        for k in range(1, grp):
            for c, part in enumerate((mine, theirs)):
                pairs = [(g * seq + q, (g ^ k) * seq + (q ^ c)) for g, q in across]
                weights[kind].append(lax.ppermute(part, ("grp", "seq"), pairs))

    slots = pick_slots(assignment, group, parts, grp)
    wanted = jnp.stack([slots[0]] + [swap(slots[k], "grp", k) for k in range(1, grp)])
    states = []
    for k in range(sides):
        if k:
            other = swap(wanted, "hd", k)
        else:
            other = wanted
        states += [other, swap(other, "seq", 1)]

    quarter = width // 4
    query = cross_query[0, 0]
    queries = []
    for k, other in enumerate((0, 2, 1, 3)):
        block = lax.dynamic_slice_in_dim(query, (place ^ other) * quarter, quarter, 1)
        queries.append(block if k == 0 else swap(block, "seq", k))

    sums = []
    for kind in range(2):
        kept, sent = project(states, weights[kind], near)
        kept = kept + swap(sent, "seq", 2).astype(F32)
        bit = 4
        while bit < seq:
            come = swap(kept.astype(BF16), "seq", bit)
            bit *= 2
            if bit < seq:
                kept = kept + come.astype(F32)
        sums.append((kept, come))

    row = jnp.arange(rows * sides)
    which, source, inner = row // rows, (row % rows) // rows_side, row % rows_side
    position = source * rows_here + (which ^ side) * rows_side + inner
    served = lax.dynamic_index_in_dim(assignment, group, keepdims=False)
    length = lax.dynamic_index_in_dim(prompt_lengths, served, keepdims=False)
    bias = jnp.where(position < length, 0.0, -1e9).astype(F32)[None]

    base = spatial_attention(qkv, residual[0, 0])
    plan = []
    for here in range(2):
        sources = [0] + [(odd if (here ^ even) & 1 else even) for even, odd in steps]
        plan.append(tuple(sources.index(k) for k in range(seq)))
    moved = temporal_attention(core, plan, pieces)
    returned = [moved[0]]
    for k in range(1, seq):
        returned.append(swap(moved[k], "seq", k))

    shares = cross_weights(bias, *sums[0], queries)
    crossed = cross_values(shares, *sums[1])
    results = [crossed[0]]
    for k in range(1, 4):
        results.append(swap(crossed[k], "seq", k))
    results[1], results[2] = results[2], results[1]
    total = gather_results(place, base, results)
    return final_sum(me, total, returned)[None, None]


def solution(mesh):
    return jax.shard_map(
        block,
        mesh=mesh,
        in_specs=(
            P("grp", "seq", None, None, "hd"),
            P("grp", "seq", None, "hd"),
            P("grp", "seq", None, "hd"),
            P(None, "seq", "grp"),
            P(("grp", "seq"), None, "hd"),
            P(),
            P(),
        ),
        out_specs=P("grp", "seq", None, "hd"),
        check_vma=False,
    )
```

```python
import functools
import math

import jax
import jax.numpy as jnp
from jax import lax
from jax.experimental import pallas as pl
from jax.experimental.pallas import tpu as pltpu
from jax.sharding import PartitionSpec as P


HDIM = 128
BF16 = jnp.bfloat16
F32 = jnp.float32


MODEST = pltpu.CompilerParams(vmem_limit_bytes=24 << 20)

VMEM_SPEC = pl.BlockSpec(memory_space=pltpu.VMEM)
SMEM_SPEC = pl.BlockSpec(memory_space=pltpu.SMEM)


def on_chip(*values):
    return [pltpu.with_memory_space_constraint(v, pltpu.VMEM) for v in values]


def swap(value, axis, bits):
    pairs = [(i, i ^ bits) for i in range(lax.axis_size(axis))]
    return lax.ppermute(value, axis, pairs)


def scores_of(queries, key_rows):
    scores = lax.dot_general(queries, key_rows, (((1,), (1,)), ((), ())), preferred_element_type=F32)
    return scores * (1.0 / math.sqrt(HDIM))


def softmax(scores):
    powered = jnp.exp(scores - jnp.max(scores, axis=-1, keepdims=True))
    return (powered * (1.0 / jnp.sum(powered, axis=-1, keepdims=True))).astype(BF16)


def lanes(head):
    return slice(head * HDIM, (head + 1) * HDIM)


def block_cols(width, most=3):
    heads = width // HDIM
    return HDIM * max(n for n in range(1, most + 1) if heads % n == 0)


def prompt_kernel(scalar_ref, in_ref, out_ref):
    blocks, _, _, feats = out_ref.shape
    for j in range(blocks):
        out_ref[j] = in_ref[:, :, j * feats : (j + 1) * feats]


def prompt_blocks(states, side, sides, blocks):
    prompts, rows, width = states.shape
    rows, feats = rows // sides, width // blocks
    if feats % HDIM:
        cut = lax.dynamic_slice_in_dim(states, side * rows, rows, 1)
        return cut.reshape(prompts, rows, blocks, feats).transpose(2, 0, 1, 3)
    shape = (blocks, prompts, rows, feats)
    return pl.pallas_call(
        prompt_kernel,
        grid_spec=pltpu.PrefetchScalarGridSpec(
            num_scalar_prefetch=1,
            grid=(1,),
            in_specs=[pl.BlockSpec((prompts, rows, width), lambda j, s: (0, s[0], 0))],
            out_specs=pl.BlockSpec(shape, lambda j, s: (0, 0, 0, 0)),
        ),
        out_shape=jax.ShapeDtypeStruct(shape, BF16),
        compiler_params=MODEST,
        name="prompt_blocks",
    )(side.reshape(1), states)


def pick_kernel(assignment_ref, group_ref, parts_ref, *out_refs):
    blocks, _, rows, _ = parts_ref.shape
    for k, out_ref in enumerate(out_refs):
        slot = assignment_ref[group_ref[0] ^ k]
        for j in range(blocks):
            out_ref[j * rows : (j + 1) * rows, :] = parts_ref[j, slot]


def pick_slots(assignment, group, parts, n_grp):
    blocks, _, rows, feats = parts.shape
    if feats % HDIM:
        slots = [lax.dynamic_index_in_dim(assignment, group ^ k, keepdims=False) for k in range(n_grp)]
        cut = [lax.dynamic_index_in_dim(parts, slot, 1, keepdims=False) for slot in slots]
        return [c.reshape(blocks * rows, feats) for c in cut]
    return pl.pallas_call(
        pick_kernel,
        in_specs=[SMEM_SPEC, SMEM_SPEC, VMEM_SPEC],
        out_specs=[VMEM_SPEC] * n_grp,
        out_shape=[pltpu.VMEM((blocks * rows, feats), BF16)] * n_grp,
        compiler_params=MODEST,
        name="pick_slots",
    )(assignment, group.reshape(1), *on_chip(parts))


def project_kernel(n_rows, places, scalar_ref, *refs):
    near = scalar_ref[0]
    state_refs = refs[: 2 * n_rows]
    kept_ref, sent_ref = refs[-2:]
    weight_refs = refs[2 * n_rows : -2]
    rows, cols = state_refs[0].shape[1], kept_ref.shape[1]

    def product(i, start):
        total = None
        for (core, group, first), weight_ref in zip(places, weight_refs):
            state = state_refs[2 * i + core][group, :, first : first + weight_ref.shape[0]]
            weight = weight_ref[:, pl.ds(pl.multiple_of(start, HDIM), cols)]
            part = jnp.dot(state, weight, preferred_element_type=F32)
            total = part if total is None else total + part
        return total

    for i in range(n_rows):
        sent_ref[i * rows : (i + 1) * rows, :] = product(i, (1 - near) * cols).astype(BF16)
    for i in range(n_rows):
        kept_ref[i * rows : (i + 1) * rows, :] = product(i, near * cols)


def project(states, weights, near):
    _, rows, _ = states[0].shape
    n_rows = len(states) // 2
    places, arrays = zip(*weights)
    shape = (n_rows * rows, arrays[0].shape[1] // 2)
    return pl.pallas_call(
        functools.partial(project_kernel, n_rows, places),
        in_specs=[SMEM_SPEC] + [VMEM_SPEC] * (len(states) + len(arrays)),
        out_specs=[VMEM_SPEC] * 2,
        out_shape=[pltpu.HBM(shape, F32), pltpu.VMEM(shape, BF16)],
        compiler_params=MODEST,
        name="project",
    )(near.reshape(1), *states, *arrays)


def spatial_kernel(qkv_ref, residual_ref, out_ref):
    for head in range(out_ref.shape[1] // HDIM):
        at = lanes(head)
        weights = softmax(scores_of(qkv_ref[0, :, at], qkv_ref[1, :, at]))
        result = jnp.dot(weights, qkv_ref[2, :, at], preferred_element_type=F32)
        out_ref[:, at] = residual_ref[:, at].astype(F32) + result


def spatial_attention(qkv, residual):
    _, tokens, width = qkv.shape
    cols = block_cols(width)
    return pl.pallas_call(
        spatial_kernel,
        grid=(width // cols,),
        in_specs=[
            pl.BlockSpec((3, tokens, cols), lambda j: (0, 0, j)),
            pl.BlockSpec((tokens, cols), lambda j: (0, j)),
        ],
        out_specs=pl.BlockSpec((tokens, cols), lambda j: (0, j)),
        out_shape=pltpu.HBM((tokens, width), F32),
        compiler_params=MODEST,
        name="spatial",
    )(qkv, residual)


def temporal_kernel(plan, scalar_ref, *refs):
    frames = len(plan[0])
    frame_refs, out_refs = refs[:frames], refs[frames:]
    _, tokens, cols = frame_refs[0].shape
    rows = frames * tokens
    row_token = lax.rem(lax.broadcasted_iota(jnp.int32, (rows, rows), 0), tokens)
    col_token = lax.rem(lax.broadcasted_iota(jnp.int32, (rows, rows), 1), tokens)
    same = row_token == col_token
    even = scalar_ref[0] == 0
    for head in range(cols // HDIM):
        at = lanes(head)
        query, key_rows, values = (
            jnp.concatenate([r[i, :, at] for r in frame_refs], axis=0) for i in range(3)
        )
        weights = softmax(jnp.where(same, scores_of(query, key_rows), -jnp.inf))
        result = jnp.dot(weights, values, preferred_element_type=F32)
        parts = [result[j * tokens : (j + 1) * tokens] for j in range(frames)]
        for out_ref, first, second in zip(out_refs, *plan):
            part = parts[first] if first == second else jnp.where(even, parts[first], parts[second])
            out_ref[:, at] = part.astype(BF16)


def temporal_attention(core, plan, pieces):
    _, tokens, width = pieces[0].shape
    cols = block_cols(width)
    return pl.pallas_call(
        functools.partial(temporal_kernel, plan),
        grid_spec=pltpu.PrefetchScalarGridSpec(
            num_scalar_prefetch=1,
            grid=(width // cols,),
            in_specs=[pl.BlockSpec((3, tokens, cols), lambda j, s: (0, 0, j))] * len(pieces),
            out_specs=[pl.BlockSpec((tokens, cols), lambda j, s: (0, j))] * len(pieces),
        ),
        out_shape=[jax.ShapeDtypeStruct((tokens, width), BF16)] * len(pieces),
        compiler_params=MODEST,
        name="temporal",
    )(core.reshape(1), *pieces)


def weigh_kernel(sides, rows_side, scalar_ref, assignment_ref, length_ref, kept_ref, come_ref, *refs):
    query_refs, out_ref = refs[:-1], refs[-1]
    group, side = scalar_ref[0], scalar_ref[1]
    length = length_ref[assignment_ref[group]]
    total = kept_ref.shape[0]
    row = lax.broadcasted_iota(jnp.int32, (1, total), 1)
    each = total // sides
    which, inner = lax.div(row, each), lax.rem(row, each)
    source, inner = lax.div(inner, rows_side), lax.rem(inner, rows_side)
    position = (source * sides + (which ^ side)) * rows_side + inner
    bias = jnp.where(position < length, 0.0, -1e9).astype(F32)
    for head in range(out_ref.shape[0]):
        at = lanes(head)
        key_rows = (kept_ref[:, at] + come_ref[:, at].astype(F32)).astype(BF16)
        for j, query_ref in enumerate(query_refs):
            out_ref[head, j] = softmax(scores_of(query_ref[:, at], key_rows) + bias)


def cross_weights(place, assignment, lengths, sides, rows_side, kept, come, queries):
    rows, width = kept.shape
    tokens = queries[0].shape[0]
    return pl.pallas_call(
        functools.partial(weigh_kernel, sides, rows_side),
        in_specs=[SMEM_SPEC] * 3 + [VMEM_SPEC] * (2 + len(queries)),
        out_specs=VMEM_SPEC,
        out_shape=pltpu.VMEM((width // HDIM, len(queries), tokens, rows), BF16),
        compiler_params=MODEST,
        name="cross_weights",
    )(place, assignment, lengths, kept, *on_chip(come), *queries)


def value_kernel(weight_ref, kept_ref, come_ref, *out_refs):
    for head in range(weight_ref.shape[0]):
        at = lanes(head)
        values = (kept_ref[:, at] + come_ref[:, at].astype(F32)).astype(BF16)
        for j, out_ref in enumerate(out_refs):
            result = jnp.dot(weight_ref[head, j], values, preferred_element_type=F32)
            out_ref[:, at] = result.astype(out_ref.dtype)


def cross_values(weights, kept, come):
    _, width = kept.shape
    _, count, tokens, _ = weights.shape
    return pl.pallas_call(
        value_kernel,
        in_specs=[VMEM_SPEC] * 3,
        out_specs=[VMEM_SPEC] * count,
        out_shape=[pltpu.VMEM((tokens, width), F32)]
        + [pltpu.VMEM((tokens, width), BF16)] * (count - 1),
        compiler_params=MODEST,
        name="cross_values",
    )(*on_chip(weights), kept, *on_chip(come))


def gather_kernel(scalar_ref, base_ref, *refs):
    piece_refs, out_ref = refs[:-1], refs[-1]
    for j, piece_ref in enumerate(piece_refs):

        @pl.when(pl.program_id(0) == j)
        def _(piece_ref=piece_ref):
            out_ref[...] = base_ref[...] + piece_ref[...].astype(F32)


def gather_results(place, base, pieces):
    tokens, width = base.shape
    cols = width // len(pieces)
    side = pl.BlockSpec((tokens, cols), lambda j, s: (0, j ^ s[0]))
    return pl.pallas_call(
        gather_kernel,
        grid_spec=pltpu.PrefetchScalarGridSpec(
            num_scalar_prefetch=1,
            grid=(len(pieces),),
            in_specs=[side] + [VMEM_SPEC] * len(pieces),
            out_specs=side,
        ),
        out_shape=pltpu.VMEM(base.shape, F32),
        compiler_params=MODEST,
        name="gather_results",
    )(place.reshape(1), base, *on_chip(*pieces))


def final_kernel(scalar_ref, total_ref, *refs):
    piece_refs, out_ref = refs[:-1], refs[-1]
    rows = piece_refs[0].shape[0]
    for k, piece_ref in enumerate(piece_refs):
        at = pl.ds(pl.multiple_of((scalar_ref[0] ^ k) * rows, rows), rows)
        out_ref[at, :] = (total_ref[at, :] + piece_ref[...].astype(F32)).astype(BF16)


def final_sum(me, total, pieces):
    return pl.pallas_call(
        final_kernel,
        in_specs=[SMEM_SPEC] + [VMEM_SPEC] * (1 + len(pieces)),
        out_specs=VMEM_SPEC,
        out_shape=jax.ShapeDtypeStruct(total.shape, BF16),
        compiler_params=MODEST,
        name="final",
    )(me.reshape(1), *on_chip(total, *pieces))


def temporal_plan(seq):
    if seq != 8:
        return [(k, k) for k in range(seq - 1, 0, -1)]
    return [(6, 2), (2, 6), (7, 3), (3, 7), (4, 4), (5, 5), (1, 1)]


def block(latent_qkv, cross_query, residual, prompt_states, kv_weight, prompt_lengths, assignment):
    tokens, width = cross_query.shape[2:]
    seq, grp, sides = (lax.axis_size(name) for name in ("seq", "grp", "hd"))
    me, group, side = (lax.axis_index(name) for name in ("seq", "grp", "hd"))
    core, near = me & 1, (me >> 1) & 1
    place = core * 2 + near
    feats = kv_weight.shape[0]
    _, rows_here, _ = prompt_states.shape
    rows_side = rows_here // sides

    parts = prompt_blocks(prompt_states, side, sides, seq)
    parts = lax.all_to_all(parts, "seq", 0, 0, tiled=True)

    qkv = latent_qkv[0, 0].transpose(1, 0, 2)
    share = tokens // seq
    steps = temporal_plan(seq)
    pieces = [lax.dynamic_slice_in_dim(qkv, me * share, share, 1)]
    held = qkv
    for number, (even, odd) in enumerate(steps):
        target = me ^ jnp.where(core == 0, even, odd)
        if number == 2:
            held, blocks = lax.optimization_barrier((qkv, blocks))
        block = lax.dynamic_slice_in_dim(held, target * share, share, 1)
        blocks = [block] if number == 0 else blocks + [block]
    for number, (even, odd) in enumerate(steps):
        pairs = [(i, i ^ (odd if i & 1 else even)) for i in range(seq)]
        pieces.append(lax.ppermute(blocks[number], "seq", pairs))

    half = width // 2
    cut = feats // 2 if feats % (2 * HDIM) == 0 else 0
    across = [(g, q) for g in range(grp) for q in range(seq)]

    def halves(source, kind, first, count):
        parts = (
            lax.dynamic_slice(source, (kind, first, c * half), (1, count, half)) for c in (core, 1 - core)
        )
        return tuple(part.reshape(count, half) for part in parts)

    early = []
    if cut:
        for k in range(1, grp):
            early.append(swap(kv_weight[:cut], "grp", k))
    planes = lax.optimization_barrier(kv_weight.transpose(1, 0, 2))
    weights, later = [], planes
    for kind in range(2):
        weights.append([])
        mine, theirs = halves(later, kind, cut, feats - cut)
        for k in range(1, grp):
            for c, part in enumerate((mine, theirs)):
                pairs = [(g * seq + q, (g ^ k) * seq + (q ^ c)) for g, q in across]
                weights[kind].append(((c, k, cut), lax.ppermute(part, ("grp", "seq"), pairs)))
        later, _ = lax.optimization_barrier((later, (mine, theirs)))
    for kind in range(2):
        mine, theirs = halves(later, kind, 0, feats)
        weights[kind] += [((0, 0, 0), mine), ((1, 0, 0), swap(theirs, "seq", 1))]
    for k, come in enumerate(early, 1):
        come = lax.optimization_barrier(come.transpose(1, 0, 2))
        for kind in range(2):
            mine, theirs = halves(come, kind, 0, cut)
            weights[kind] += [((0, k, 0), mine), ((1, k, 0), swap(theirs, "seq", 1))]

    slots = pick_slots(assignment, group, parts, grp)
    wanted = jnp.stack([slots[0]] + [swap(slots[k], "grp", k) for k in range(1, grp)])
    states = []
    for k in range(sides):
        if k:
            other = swap(wanted, "hd", k)
        else:
            other = wanted
        states += [other, swap(other, "seq", 1)]

    quarter = width // 4
    query = cross_query[0, 0]
    queries = []
    for k, other in enumerate((0, 2, 1, 3)):
        block = lax.dynamic_slice_in_dim(query, (place ^ other) * quarter, quarter, 1)
        queries.append(block if k == 0 else swap(block, "seq", k))

    sums = []
    for kind in range(2):
        kept, sent = project(states, weights[kind], near)
        kept = kept + swap(sent, "seq", 2).astype(F32)
        bit = 4
        while bit < seq:
            come = swap(kept.astype(BF16), "seq", bit)
            bit *= 2
            if bit < seq:
                kept = kept + come.astype(F32)
        sums.append((kept, come))

    base = spatial_attention(qkv, residual[0, 0])
    plan = []
    for here in range(2):
        sources = [0] + [(odd if (here ^ even) & 1 else even) for even, odd in steps]
        plan.append(tuple(sources.index(k) for k in range(seq)))
    moved = temporal_attention(core, plan, pieces)
    returned = [moved[0]]
    for k in range(1, seq):
        returned.append(swap(moved[k], "seq", k))

    device = jnp.stack([group, side]).astype(jnp.int32)
    shares = cross_weights(device, assignment, prompt_lengths, sides, rows_side, *sums[0], queries)
    crossed = cross_values(shares, *sums[1])
    results = [crossed[0]]
    for k in range(1, 4):
        results.append(swap(crossed[k], "seq", k))
    results[1], results[2] = results[2], results[1]
    total = gather_results(place, base, results)
    return final_sum(me, total, returned)[None, None]


def solution(mesh):
    return jax.shard_map(
        block,
        mesh=mesh,
        in_specs=(
            P("grp", "seq", None, None, "hd"),
            P("grp", "seq", None, "hd"),
            P("grp", "seq", None, "hd"),
            P(None, "seq", "grp"),
            P(("grp", "seq"), None, "hd"),
            P(),
            P(),
        ),
        out_specs=P("grp", "seq", None, "hd"),
        check_vma=False,
    )
```

```python
import functools
import math

import jax
import jax.numpy as jnp
from jax import lax
from jax.experimental import pallas as pl
from jax.experimental.pallas import tpu as pltpu
from jax.sharding import PartitionSpec as P


HDIM = 128
BF16 = jnp.bfloat16
F32 = jnp.float32


MODEST = pltpu.CompilerParams(vmem_limit_bytes=24 << 20)

VMEM_SPEC = pl.BlockSpec(memory_space=pltpu.VMEM)
SMEM_SPEC = pl.BlockSpec(memory_space=pltpu.SMEM)


def on_chip(*values):
    return [pltpu.with_memory_space_constraint(v, pltpu.VMEM) for v in values]


def swap(value, axis, bits):
    pairs = [(i, i ^ bits) for i in range(lax.axis_size(axis))]
    return lax.ppermute(value, axis, pairs)


def scores_of(queries, key_rows):
    scores = lax.dot_general(queries, key_rows, (((1,), (1,)), ((), ())), preferred_element_type=F32)
    return scores * (1.0 / math.sqrt(HDIM))


def softmax(scores):
    powered = jnp.exp(scores - jnp.max(scores, axis=-1, keepdims=True))
    return (powered * (1.0 / jnp.sum(powered, axis=-1, keepdims=True))).astype(BF16)


def lanes(head):
    return slice(head * HDIM, (head + 1) * HDIM)


def block_cols(width, most=3):
    heads = width // HDIM
    return HDIM * max(n for n in range(1, most + 1) if heads % n == 0)


def prompt_kernel(scalar_ref, in_ref, out_ref):
    blocks, _, _, feats = out_ref.shape
    for j in range(blocks):
        out_ref[j] = in_ref[:, :, j * feats : (j + 1) * feats]


def prompt_blocks(states, side, sides, blocks):
    prompts, rows, width = states.shape
    rows, feats = rows // sides, width // blocks
    if feats % HDIM:
        cut = lax.dynamic_slice_in_dim(states, side * rows, rows, 1)
        return cut.reshape(prompts, rows, blocks, feats).transpose(2, 0, 1, 3)
    shape = (blocks, prompts, rows, feats)
    return pl.pallas_call(
        prompt_kernel,
        grid_spec=pltpu.PrefetchScalarGridSpec(
            num_scalar_prefetch=1,
            grid=(1,),
            in_specs=[pl.BlockSpec((prompts, rows, width), lambda j, s: (0, s[0], 0))],
            out_specs=pl.BlockSpec(shape, lambda j, s: (0, 0, 0, 0)),
        ),
        out_shape=jax.ShapeDtypeStruct(shape, BF16),
        compiler_params=MODEST,
        name="prompt_blocks",
    )(side.reshape(1), states)


def pick_kernel(assignment_ref, group_ref, parts_ref, *out_refs):
    blocks, _, rows, _ = parts_ref.shape
    for k, out_ref in enumerate(out_refs):
        slot = assignment_ref[group_ref[0] ^ k]
        for j in range(blocks):
            out_ref[j * rows : (j + 1) * rows, :] = parts_ref[j, slot]


def pick_slots(assignment, group, parts, n_grp):
    blocks, _, rows, feats = parts.shape
    if feats % HDIM:
        slots = [lax.dynamic_index_in_dim(assignment, group ^ k, keepdims=False) for k in range(n_grp)]
        cut = [lax.dynamic_index_in_dim(parts, slot, 1, keepdims=False) for slot in slots]
        return [c.reshape(blocks * rows, feats) for c in cut]
    return pl.pallas_call(
        pick_kernel,
        in_specs=[SMEM_SPEC, SMEM_SPEC, VMEM_SPEC],
        out_specs=[VMEM_SPEC] * n_grp,
        out_shape=[pltpu.VMEM((blocks * rows, feats), BF16)] * n_grp,
        compiler_params=MODEST,
        name="pick_slots",
    )(assignment, group.reshape(1), *on_chip(parts))


def project_kernel(n_rows, places, scalar_ref, *refs):
    near = scalar_ref[0]
    state_refs = refs[: 2 * n_rows]
    kept_ref, sent_ref = refs[-2:]
    weight_refs = refs[2 * n_rows : -2]
    rows, cols = state_refs[0].shape[1], kept_ref.shape[1]

    def product(i, start):
        total = None
        for (core, group, first), weight_ref in zip(places, weight_refs):
            state = state_refs[2 * i + core][group, :, first : first + weight_ref.shape[0]]
            weight = weight_ref[:, pl.ds(pl.multiple_of(start, HDIM), cols)]
            part = jnp.dot(state, weight, preferred_element_type=F32)
            total = part if total is None else total + part
        return total

    for i in range(n_rows):
        sent_ref[i * rows : (i + 1) * rows, :] = product(i, (1 - near) * cols).astype(BF16)
    for i in range(n_rows):
        kept_ref[i * rows : (i + 1) * rows, :] = product(i, near * cols)


def project(states, weights, near):
    _, rows, _ = states[0].shape
    n_rows = len(states) // 2
    places = [place for place, _ in weights]
    arrays = [on_chip(array)[0] if place[1] else array for place, array in weights]
    shape = (n_rows * rows, arrays[0].shape[1] // 2)
    return pl.pallas_call(
        functools.partial(project_kernel, n_rows, places),
        in_specs=[SMEM_SPEC] + [VMEM_SPEC] * (len(states) + len(arrays)),
        out_specs=[VMEM_SPEC] * 2,
        out_shape=[pltpu.HBM(shape, F32), pltpu.VMEM(shape, BF16)],
        compiler_params=MODEST,
        name="project",
    )(near.reshape(1), *on_chip(*states), *arrays)


def spatial_kernel(qkv_ref, residual_ref, out_ref):
    for head in range(out_ref.shape[1] // HDIM):
        at = lanes(head)
        weights = softmax(scores_of(qkv_ref[0, :, at], qkv_ref[1, :, at]))
        result = jnp.dot(weights, qkv_ref[2, :, at], preferred_element_type=F32)
        out_ref[:, at] = residual_ref[:, at].astype(F32) + result


def spatial_attention(qkv, residual):
    _, tokens, width = qkv.shape
    cols = block_cols(width)
    return pl.pallas_call(
        spatial_kernel,
        grid=(width // cols,),
        in_specs=[
            pl.BlockSpec((3, tokens, cols), lambda j: (0, 0, j)),
            pl.BlockSpec((tokens, cols), lambda j: (0, j)),
        ],
        out_specs=pl.BlockSpec((tokens, cols), lambda j: (0, j)),
        out_shape=pltpu.HBM((tokens, width), F32),
        compiler_params=MODEST,
        name="spatial",
    )(qkv, residual)


def temporal_kernel(plan, scalar_ref, *refs):
    frames = len(plan[0])
    frame_refs, out_refs = refs[:frames], refs[frames:]
    _, tokens, cols = frame_refs[0].shape
    rows = frames * tokens
    row_token = lax.rem(lax.broadcasted_iota(jnp.int32, (rows, rows), 0), tokens)
    col_token = lax.rem(lax.broadcasted_iota(jnp.int32, (rows, rows), 1), tokens)
    same = row_token == col_token
    even = scalar_ref[0] == 0
    for head in range(cols // HDIM):
        at = lanes(head)
        query, key_rows, values = (
            jnp.concatenate([r[i, :, at] for r in frame_refs], axis=0) for i in range(3)
        )
        weights = softmax(jnp.where(same, scores_of(query, key_rows), -jnp.inf))
        result = jnp.dot(weights, values, preferred_element_type=F32)
        parts = [result[j * tokens : (j + 1) * tokens] for j in range(frames)]
        for out_ref, first, second in zip(out_refs, *plan):
            part = parts[first] if first == second else jnp.where(even, parts[first], parts[second])
            out_ref[:, at] = part.astype(BF16)


def temporal_attention(core, plan, pieces):
    _, tokens, width = pieces[0].shape
    cols = block_cols(width)
    return pl.pallas_call(
        functools.partial(temporal_kernel, plan),
        grid_spec=pltpu.PrefetchScalarGridSpec(
            num_scalar_prefetch=1,
            grid=(width // cols,),
            in_specs=[pl.BlockSpec((3, tokens, cols), lambda j, s: (0, 0, j))] * len(pieces),
            out_specs=[pl.BlockSpec((tokens, cols), lambda j, s: (0, j))] * len(pieces),
        ),
        out_shape=[jax.ShapeDtypeStruct((tokens, width), BF16)] * len(pieces),
        compiler_params=MODEST,
        name="temporal",
    )(core.reshape(1), *pieces)


def weigh_kernel(sides, rows_side, scalar_ref, assignment_ref, length_ref, kept_ref, come_ref, *refs):
    query_refs, out_ref = refs[:-1], refs[-1]
    group, side = scalar_ref[0], scalar_ref[1]
    length = length_ref[assignment_ref[group]]
    total = kept_ref.shape[0]
    row = lax.broadcasted_iota(jnp.int32, (1, total), 1)
    each = total // sides
    which, inner = lax.div(row, each), lax.rem(row, each)
    source, inner = lax.div(inner, rows_side), lax.rem(inner, rows_side)
    position = (source * sides + (which ^ side)) * rows_side + inner
    bias = jnp.where(position < length, 0.0, -1e9).astype(F32)
    for head in range(out_ref.shape[0]):
        at = lanes(head)
        key_rows = (kept_ref[:, at] + come_ref[:, at].astype(F32)).astype(BF16)
        for j, query_ref in enumerate(query_refs):
            out_ref[head, j] = softmax(scores_of(query_ref[:, at], key_rows) + bias)


def cross_weights(place, assignment, lengths, sides, rows_side, kept, come, queries):
    rows, width = kept.shape
    tokens = queries[0].shape[0]
    return pl.pallas_call(
        functools.partial(weigh_kernel, sides, rows_side),
        in_specs=[SMEM_SPEC] * 3 + [VMEM_SPEC] * (2 + len(queries)),
        out_specs=VMEM_SPEC,
        out_shape=pltpu.VMEM((width // HDIM, len(queries), tokens, rows), BF16),
        compiler_params=MODEST,
        name="cross_weights",
    )(place, assignment, lengths, kept, *on_chip(come), *queries)


def value_kernel(weight_ref, kept_ref, come_ref, *out_refs):
    for head in range(weight_ref.shape[0]):
        at = lanes(head)
        values = (kept_ref[:, at] + come_ref[:, at].astype(F32)).astype(BF16)
        for j, out_ref in enumerate(out_refs):
            result = jnp.dot(weight_ref[head, j], values, preferred_element_type=F32)
            out_ref[:, at] = result.astype(out_ref.dtype)


def cross_values(weights, kept, come):
    _, width = kept.shape
    _, count, tokens, _ = weights.shape
    return pl.pallas_call(
        value_kernel,
        in_specs=[VMEM_SPEC] * 3,
        out_specs=[VMEM_SPEC] * count,
        out_shape=[pltpu.VMEM((tokens, width), F32)]
        + [pltpu.VMEM((tokens, width), BF16)] * (count - 1),
        compiler_params=MODEST,
        name="cross_values",
    )(*on_chip(weights), kept, *on_chip(come))


def gather_kernel(scalar_ref, base_ref, *refs):
    piece_refs, out_ref = refs[:-1], refs[-1]
    for j, piece_ref in enumerate(piece_refs):

        @pl.when(pl.program_id(0) == j)
        def _(piece_ref=piece_ref):
            out_ref[...] = base_ref[...] + piece_ref[...].astype(F32)


def gather_results(place, base, pieces):
    tokens, width = base.shape
    cols = width // len(pieces)
    side = pl.BlockSpec((tokens, cols), lambda j, s: (0, j ^ s[0]))
    return pl.pallas_call(
        gather_kernel,
        grid_spec=pltpu.PrefetchScalarGridSpec(
            num_scalar_prefetch=1,
            grid=(len(pieces),),
            in_specs=[side] + [VMEM_SPEC] * len(pieces),
            out_specs=side,
        ),
        out_shape=pltpu.VMEM(base.shape, F32),
        compiler_params=MODEST,
        name="gather_results",
    )(place.reshape(1), base, *on_chip(*pieces))


def final_kernel(scalar_ref, total_ref, *refs):
    piece_refs, out_ref = refs[:-1], refs[-1]
    rows = piece_refs[0].shape[0]
    for k, piece_ref in enumerate(piece_refs):
        at = pl.ds(pl.multiple_of((scalar_ref[0] ^ k) * rows, rows), rows)
        out_ref[at, :] = (total_ref[at, :] + piece_ref[...].astype(F32)).astype(BF16)


def final_sum(me, total, pieces):
    return pl.pallas_call(
        final_kernel,
        in_specs=[SMEM_SPEC] + [VMEM_SPEC] * (1 + len(pieces)),
        out_specs=VMEM_SPEC,
        out_shape=jax.ShapeDtypeStruct(total.shape, BF16),
        compiler_params=MODEST,
        name="final",
    )(me.reshape(1), *on_chip(total, *pieces))


def temporal_plan(seq):
    if seq != 8:
        return [(k, k) for k in range(seq - 1, 0, -1)]
    return [(6, 2), (2, 6), (7, 3), (3, 7), (4, 4), (5, 5), (1, 1)]


def block(latent_qkv, cross_query, residual, prompt_states, kv_weight, prompt_lengths, assignment):
    tokens, width = cross_query.shape[2:]
    seq, grp, sides = (lax.axis_size(name) for name in ("seq", "grp", "hd"))
    me, group, side = (lax.axis_index(name) for name in ("seq", "grp", "hd"))
    core, near = me & 1, (me >> 1) & 1
    place = core * 2 + near
    feats = kv_weight.shape[0]
    _, rows_here, _ = prompt_states.shape
    rows_side = rows_here // sides

    parts = prompt_blocks(prompt_states, side, sides, seq)
    parts = lax.all_to_all(parts, "seq", 0, 0, tiled=True)

    qkv = latent_qkv[0, 0].transpose(1, 0, 2)
    share = tokens // seq
    steps = temporal_plan(seq)
    pieces = [lax.dynamic_slice_in_dim(qkv, me * share, share, 1)]
    held = qkv
    for number, (even, odd) in enumerate(steps):
        target = me ^ jnp.where(core == 0, even, odd)
        if number == 2:
            held, blocks = lax.optimization_barrier((qkv, blocks))
        block = lax.dynamic_slice_in_dim(held, target * share, share, 1)
        blocks = [block] if number == 0 else blocks + [block]
    for number, (even, odd) in enumerate(steps):
        pairs = [(i, i ^ (odd if i & 1 else even)) for i in range(seq)]
        pieces.append(lax.ppermute(blocks[number], "seq", pairs))

    half = width // 2
    cut = feats // 2 if feats % (2 * HDIM) == 0 else 0
    across = [(g, q) for g in range(grp) for q in range(seq)]

    def halves(source, kind, first, count):
        parts = (
            lax.dynamic_slice(source, (kind, first, c * half), (1, count, half)) for c in (core, 1 - core)
        )
        return tuple(part.reshape(count, half) for part in parts)

    early = []
    if cut:
        for k in range(1, grp):
            early.append(swap(kv_weight[:cut], "grp", k))
    planes = lax.optimization_barrier(kv_weight.transpose(1, 0, 2))
    weights, later = [], planes
    for kind in range(2):
        weights.append([])
        mine, theirs = halves(later, kind, cut, feats - cut)
        for k in range(1, grp):
            for c, part in enumerate((mine, theirs)):
                pairs = [(g * seq + q, (g ^ k) * seq + (q ^ c)) for g, q in across]
                weights[kind].append(((c, k, cut), lax.ppermute(part, ("grp", "seq"), pairs)))
        later, _ = lax.optimization_barrier((later, (mine, theirs)))
    for kind in range(2):
        mine, theirs = halves(later, kind, 0, feats)
        weights[kind] += [((0, 0, 0), mine), ((1, 0, 0), swap(theirs, "seq", 1))]
    for k, come in enumerate(early, 1):
        come = lax.optimization_barrier(come.transpose(1, 0, 2))
        for kind in range(2):
            mine, theirs = halves(come, kind, 0, cut)
            weights[kind] += [((0, k, 0), mine), ((1, k, 0), swap(theirs, "seq", 1))]

    slots = pick_slots(assignment, group, parts, grp)
    wanted = jnp.stack([slots[0]] + [swap(slots[k], "grp", k) for k in range(1, grp)])
    states = []
    for k in range(sides):
        if k:
            other = swap(wanted, "hd", k)
        else:
            other = wanted
        states += [other, swap(other, "seq", 1)]

    quarter = width // 4
    query = cross_query[0, 0]
    queries = []
    for k, other in enumerate((0, 2, 1, 3)):
        block = lax.dynamic_slice_in_dim(query, (place ^ other) * quarter, quarter, 1)
        queries.append(block if k == 0 else swap(block, "seq", k))

    sums = []
    for kind in range(2):
        kept, sent = project(states, weights[kind], near)
        kept = kept + swap(sent, "seq", 2).astype(F32)
        bit = 4
        while bit < seq:
            come = swap(kept.astype(BF16), "seq", bit)
            bit *= 2
            if bit < seq:
                kept = kept + come.astype(F32)
        sums.append((kept, come))

    base = spatial_attention(qkv, residual[0, 0])
    plan = []
    for here in range(2):
        sources = [0] + [(odd if (here ^ even) & 1 else even) for even, odd in steps]
        plan.append(tuple(sources.index(k) for k in range(seq)))
    moved = temporal_attention(core, plan, pieces)
    returned = [moved[0]]
    for k in range(1, seq):
        returned.append(swap(moved[k], "seq", k))

    device = jnp.stack([group, side]).astype(jnp.int32)
    shares = cross_weights(device, assignment, prompt_lengths, sides, rows_side, *sums[0], queries)
    crossed = cross_values(shares, *sums[1])
    results = [crossed[0]]
    for k in range(1, 4):
        results.append(swap(crossed[k], "seq", k))
    results[1], results[2] = results[2], results[1]
    total = gather_results(place, base, results)
    return final_sum(me, total, returned)[None, None]


def solution(mesh):
    return jax.shard_map(
        block,
        mesh=mesh,
        in_specs=(
            P("grp", "seq", None, None, "hd"),
            P("grp", "seq", None, "hd"),
            P("grp", "seq", None, "hd"),
            P(None, "seq", "grp"),
            P(("grp", "seq"), None, "hd"),
            P(),
            P(),
        ),
        out_specs=P("grp", "seq", None, "hd"),
        check_vma=False,
    )
```
